512 devices in a mesh: tile: 64 (over z_hi, y, core), dp: 8 (over z_lo, x).
Axes of the slice: x: 4, y: 8, z: 8 (z_hi: 4, z_lo: 2; z = z_hi * 2 + z_lo), core: 2. Of those that a mesh axis runs over, the one named last changes fastest.
Arguments:
- fields: bfloat16 [8, 768, 64, 128], P('dp', 'tile'), may hold values from -6 to 6
- cotangent: bfloat16 [8, 768, 64, 128], P('dp', 'tile'), may hold values from -6 to 6
- face_flip: int32 [12], replicated, may hold values from 0 to 1
- kernel: bfloat16 [2, 49, 128], replicated, may hold values from -0.875 to 0.875
- ln_gain: float32 [2, 128], replicated, may hold values from 0.25 to 1.75
- weight_in: bfloat16 [2, 128, 512], replicated, may hold values from -0.5 to 0.5
- bias_in: float32 [2, 512], replicated, may hold values from -3 to 3
- weight_out: bfloat16 [2, 512, 128], replicated, may hold values from -0.25 to 0.25
- layer_scale: float32 [2, 128], replicated, may hold values from 0.25 to 1
Outputs:
- result: bfloat16 [8, 768, 64, 128], P('dp', 'tile')
- grad_input: bfloat16 [8, 768, 64, 128], P('dp', 'tile')
- grad_kernel: float32 [2, 49, 128], P(None, None, 'dp')
- grad_gain: float32 [2, 128], P(None, 'dp')
- grad_weight_in: float32 [2, 128, 512], P(None, 'dp')
- grad_bias_in: float32 [2, 512], P(None, 'dp')
- grad_weight_out: float32 [2, 512, 128], P(None, 'dp')
- grad_scale: float32 [2, 128], P(None, 'dp')
The draws below stay inside these ranges and needn't reach their ends.
All inputs are finite; a program needn't handle non-finite values.
Results may differ from the reference program's by a relative error of at most 0.018.
Values may be sent and summed in bfloat16 or wider, within the bound.
No kernel may reach another device: no remote copies, remote signals or barrier semaphores. Data moves between devices by JAX's collectives and lax.ppermute only.
A program may use at most 64 MiB of HBM per device.

```python
import math
import jax
import jax.numpy as jnp
from jax import lax

C = 128
HID = 512
KS = 7
BLOCKS = 2
F = 64
SAMPLES = 8
CELLS = 393216


def touch_ends(result, own_key, least, largest):
    extent = result.shape
    index_at = [jax.random.randint(jax.random.fold_in(own_key, axis), (), 0, extent[axis]) for axis in range(len(extent))]
    result = result.at[tuple(index_at)].set(least)
    longest = extent.index(max(extent))
    index_at[longest] = (index_at[longest] + 1) % extent[longest]
    return result.at[tuple(index_at)].set(largest)


def block_levels(own_key, extent, pieces, smallest, high):
    level, own = 1.0, jax.random.fold_in(own_key, 6)
    for position, blocks in pieces:
        steps = jnp.exp(jax.random.uniform(jax.random.fold_in(own, position), (blocks,), jnp.float32, smallest / len(pieces), high / len(pieces)))
        level = level * jnp.repeat(steps, extent[position] // blocks).reshape([-1 if axis == position else 1 for axis in range(len(extent))])
    return level


def bell_draw(key, extent, scale, limit, cuts=(), held_as=jnp.bfloat16):
    loudness = block_levels(key, extent, cuts, -0.22, 0.18) if cuts else 1.0
    array = jax.random.normal(key, extent, jnp.float32) * scale * loudness
    return jnp.minimum(jnp.maximum(array, -limit), limit).astype(held_as)


def setup_inputs(seed: int = 0) -> dict:
    splits = jax.random.split(jax.random.key(seed), 10)
    return {
        "fields": bell_draw(splits[0], (SAMPLES, 12 * F, F, C), 1.0, 6.0, ((0, 8), (1, 64))),
        "cotangent": bell_draw(splits[1], (SAMPLES, 12 * F, F, C), 1.0, 6.0, ((0, 8), (1, 64))),
        "face_flip": touch_ends(jax.random.randint(splits[2], (12,), 0, 2), jax.random.fold_in(splits[2], 1), 0, 1).astype(jnp.int32),
        "kernel": bell_draw(splits[3], (BLOCKS, KS * KS, C), (KS * KS) ** -0.5, 0.875),
        "ln_gain": jnp.clip(1.0 + 0.15 * jax.random.normal(splits[4], (BLOCKS, C), jnp.float32), 0.25, 1.75),
        "weight_in": bell_draw(splits[5], (BLOCKS, C, HID), C ** -0.5, 0.5),
        "bias_in": bell_draw(splits[6], (BLOCKS, HID), 0.5, 3.0, (), jnp.float32),
        "weight_out": bell_draw(splits[7], (BLOCKS, HID, C), HID ** -0.5, 0.25),
        "layer_scale": jnp.clip(jnp.exp(jax.random.uniform(splits[8], (BLOCKS, C), jnp.float32, math.log(0.25), math.log(1.0))), 0.25, 1.0),
    }


EPSILON = 1e-06
SQRT_HALF = 0.7071067811865476
INV_ROOT_TWO_PI = 0.3989422804014327

def gelu_parts(preact):
    normal_cdf = 0.5 * (1.0 + jax.scipy.special.erf(preact * SQRT_HALF))
    return (preact * normal_cdf, normal_cdf + preact * jnp.exp(-0.5 * preact * preact) * INV_ROOT_TWO_PI)

def depthwise(padded, kernel_taps):
    return lax.conv_general_dilated(padded, kernel_taps[:, :, None, :], (1, 1), 'VALID', dimension_numbers=('NHWC', 'HWIO', 'NHWC'), feature_group_count=padded.shape[3], preferred_element_type=jnp.float32)

def tap_sums(padded_one, grad_one):
    summed = lax.conv_general_dilated(padded_one, grad_one[:, :, None, :], (1, 1), 'VALID', dimension_numbers=('NHWC', 'HWIO', 'NHWC'), feature_group_count=padded_one.shape[3], preferred_element_type=jnp.float32)
    return summed[0]

def row_flags(face_flip, row_start, count, width):
    row_ids = row_start + jnp.arange(count, dtype=jnp.int32)
    column_ids = row_ids // (3 * width)
    levels = row_ids % (3 * width) // width
    face_ids = 4 * levels + column_ids
    matches = face_ids[:, None] == jnp.arange(12, dtype=jnp.int32)[None, :]
    return lax.optimization_barrier(jnp.sum(jnp.where(matches, face_flip[None, :], 0), axis=1)) > 0

def orient(states, flipped):
    return jnp.where(flipped[:, None, None], states[:, ::-1], states)

def extend_whole(states):
    total_rows = states.shape[0]
    width = states.shape[1]
    column_rows = 3 * width
    starts = column_rows * jnp.arange(4, dtype=jnp.int32)
    offsets = jnp.arange(-3, column_rows + 3, dtype=jnp.int32)
    row_index = (starts[:, None] + offsets[None, :]) % total_rows
    with_rows = jnp.take(states, row_index.reshape(-1), axis=0).reshape(4, column_rows + 6, width, states.shape[2])
    western = jnp.roll(with_rows, 1, axis=0)[:, :, width - 3:]
    eastern = jnp.roll(with_rows, -1, axis=0)[:, :, :3]
    return jnp.concatenate([western, with_rows, eastern], axis=2)

def forward_block(states, kernel_taps, gain_row, weight_in_row, bias_row, weight_out_row, scale_row):
    channels = states.shape[2]
    padded = extend_whole(states)
    convolved = depthwise(padded, kernel_taps).reshape(-1, channels)
    average = lax.optimization_barrier(jnp.mean(convolved, axis=-1, keepdims=True))
    centered = convolved - average
    inv_std = lax.rsqrt(lax.optimization_barrier(jnp.mean(centered * centered, axis=-1, keepdims=True)) + EPSILON)
    normed = centered * inv_std
    scaled = (normed * gain_row).astype(jnp.bfloat16)
    preact = jnp.dot(scaled, weight_in_row, preferred_element_type=jnp.float32) + bias_row
    gelu_value, gelu_slope = gelu_parts(preact)
    hidden = gelu_value.astype(jnp.bfloat16)
    branch = jnp.dot(hidden, weight_out_row, preferred_element_type=jnp.float32)
    output = (states.reshape(-1, channels).astype(jnp.float32) + scale_row * branch).astype(jnp.bfloat16)
    return (output.reshape(states.shape), (padded, normed, inv_std, scaled, gelu_slope, hidden, branch))

def backward_block(upstream, saved, kernel_taps, gain_row, weight_in_row, weight_out_row, scale_row):
    padded, normed, inv_std, scaled, gelu_slope, hidden, branch = saved
    grid_shape = upstream.shape
    channels = grid_shape[2]
    width = grid_shape[1]
    up_float = upstream.reshape(-1, channels).astype(jnp.float32)
    grad_scale = lax.optimization_barrier(jnp.sum(up_float * branch, axis=0))
    grad_branch = (up_float * scale_row).astype(jnp.bfloat16)
    grad_weight_out = jnp.dot(hidden.T, grad_branch, preferred_element_type=jnp.float32)
    grad_preact = (jnp.dot(grad_branch, weight_out_row.T, preferred_element_type=jnp.float32) * gelu_slope).astype(jnp.bfloat16)
    grad_bias = lax.optimization_barrier(jnp.sum(grad_preact.astype(jnp.float32), axis=0))
    grad_weight_in = jnp.dot(scaled.T, grad_preact, preferred_element_type=jnp.float32)
    grad_scaled = jnp.dot(grad_preact, weight_in_row.T, preferred_element_type=jnp.float32)
    grad_gain = lax.optimization_barrier(jnp.sum(grad_scaled * normed, axis=0))
    grad_normed = grad_scaled * gain_row
    grad_conv = inv_std * (grad_normed - lax.optimization_barrier(jnp.mean(grad_normed, axis=-1, keepdims=True)) - normed * lax.optimization_barrier(jnp.mean(grad_normed * normed, axis=-1, keepdims=True)))
    grad_conv = grad_conv.astype(jnp.bfloat16).reshape(grid_shape)
    grad_padded = extend_whole(grad_conv)
    grad_columns = grad_conv.reshape(4, -1, width, channels)
    grad_taps = tap_sums(padded[0:1], grad_columns[0])
    for column_index in range(1, 4):
        grad_taps = grad_taps + tap_sums(padded[column_index:column_index + 1], grad_columns[column_index])
    spread = depthwise(grad_padded, kernel_taps[::-1, ::-1]).reshape(-1, channels)
    grad_field = (up_float + spread).astype(jnp.bfloat16).reshape(grid_shape)
    return (grad_field, (grad_taps.reshape(-1, channels), grad_gain, grad_weight_in, grad_bias, grad_weight_out, grad_scale))

def reference(fields, cotangent, face_flip, kernel, ln_gain, weight_in, bias_in, weight_out, layer_scale):

    def one_sample(inputs_pair):
        states, upstream = inputs_pair
        channels = states.shape[2]
        flipped = row_flags(face_flip, 0, states.shape[0], states.shape[1])
        current = orient(states, flipped)
        saved_all = []
        for layer_index in range(BLOCKS):
            kernel_taps = kernel[layer_index].reshape(KS, KS, channels)
            current, saved = forward_block(current, kernel_taps, ln_gain[layer_index], weight_in[layer_index], bias_in[layer_index], weight_out[layer_index], layer_scale[layer_index])
            saved_all.append(saved)
        output = orient(current, flipped)
        grad_field = orient(upstream, flipped)
        gradients = [None] * BLOCKS
        for layer_index in reversed(range(BLOCKS)):
            kernel_taps = kernel[layer_index].reshape(KS, KS, channels)
            grad_field, gradients[layer_index] = backward_block(grad_field, saved_all[layer_index], kernel_taps, ln_gain[layer_index], weight_in[layer_index], weight_out[layer_index], layer_scale[layer_index])
        stacked = tuple((jnp.stack([entry[member] for entry in gradients]) for member in range(6)))
        return (output, orient(grad_field, flipped), stacked)
    outputs, grad_inputs, gradients = lax.map(one_sample, (fields, cotangent))
    normalizer = 1.0 / math.sqrt(CELLS)
    totals = tuple((lax.optimization_barrier(jnp.sum(entry, axis=0)) * normalizer for entry in gradients))
    return (outputs, grad_inputs, totals[0], totals[1], totals[2], totals[3], totals[4], totals[5])
```

```python
import math

import jax
import jax.numpy as jnp
from jax import lax
from jax.sharding import PartitionSpec as P

KS = 7
TILE = ("zh", "y", "c")
DP = ("zl", "x")


EPSILON = 1e-06
SQRT_HALF = 0.7071067811865476
INV_ROOT_TWO_PI = 0.3989422804014327


def padded_2(x, sides, width):
    for axis, dim in sides:
        count, length = (lax.axis_size(axis), x.shape[dim])
        up = [(i, (i + 1) % count) for i in range(count)]
        down = [(j, i) for i, j in up]
        last = lax.slice_in_dim(x, length - width, length, axis=dim)
        initial = lax.slice_in_dim(x, 0, width, axis=dim)
        before = lax.ppermute(last, axis, up)
        after = lax.ppermute(initial, axis, down)
        x = jnp.concatenate([before, x, after], axis=dim)
    return x


def passed_along(block, axis, distance):
    devices = range(lax.axis_size(axis))
    route = [((i - distance) % len(devices), i) for i in devices]
    return lax.ppermute(block, axis, route)


def gelu_parts(preact):
    normal_cdf = 0.5 * (1.0 + jax.scipy.special.erf(preact * SQRT_HALF))
    return (
        preact * normal_cdf,
        normal_cdf + preact * jnp.exp(-0.5 * preact * preact) * INV_ROOT_TWO_PI,
    )


def depthwise(padded, kernel_taps):
    return lax.conv_general_dilated(
        padded[None],
        kernel_taps[:, :, None, :],
        (1, 1),
        "VALID",
        dimension_numbers=("NHWC", "HWIO", "NHWC"),
        feature_group_count=padded.shape[2],
        preferred_element_type=jnp.float32,
    )[0]


def tap_sums(padded, grad_conv):
    summed = lax.conv_general_dilated(
        padded[None],
        grad_conv[:, :, None, :],
        (1, 1),
        "VALID",
        dimension_numbers=("NHWC", "HWIO", "NHWC"),
        feature_group_count=padded.shape[2],
        preferred_element_type=jnp.float32,
    )
    return summed[0]


def row_flags(face_flip, row_start, count, width):
    row_ids = row_start + jnp.arange(count, dtype=jnp.int32)
    column_ids = row_ids // (3 * width)
    levels = row_ids % (3 * width) // width
    face_ids = 4 * levels + column_ids
    matches = face_ids[:, None] == jnp.arange(12, dtype=jnp.int32)[None, :]
    return jnp.sum(jnp.where(matches, face_flip[None, :], 0), axis=1) > 0


def orient(states, flipped):
    return jnp.where(flipped[:, None, None], states[:, ::-1], states)


def extend_strip(states, strip_count):
    width = states.shape[1]
    extended = padded_2(states, ((TILE, 0),), 3)
    western = passed_along(extended[:, width - 3 :], TILE, strip_count)
    eastern = passed_along(extended[:, :3], TILE, -strip_count)
    return jnp.concatenate([western, extended, eastern], axis=1)


def forward_block(
    states, kernel_taps, gain_row, weight_in_row, bias_row, weight_out_row, scale_row, strip_count
):
    channels = states.shape[2]
    padded = extend_strip(states, strip_count)
    convolved = depthwise(padded, kernel_taps).reshape(-1, channels)
    average = jnp.mean(convolved, axis=-1, keepdims=True)
    centered = convolved - average
    inv_std = lax.rsqrt(jnp.mean(centered * centered, axis=-1, keepdims=True) + EPSILON)
    normed = centered * inv_std
    scaled = (normed * gain_row).astype(jnp.bfloat16)
    preact = jnp.dot(scaled, weight_in_row, preferred_element_type=jnp.float32) + bias_row
    gelu_value, gelu_slope = gelu_parts(preact)
    hidden = gelu_value.astype(jnp.bfloat16)
    branch = jnp.dot(hidden, weight_out_row, preferred_element_type=jnp.float32)
    output = (states.reshape(-1, channels).astype(jnp.float32) + scale_row * branch).astype(
        jnp.bfloat16
    )
    return (
        output.reshape(states.shape),
        (padded, normed, inv_std, scaled, gelu_slope, hidden, branch),
    )


def backward_block(
    upstream, saved, kernel_taps, gain_row, weight_in_row, weight_out_row, scale_row, strip_count
):
    padded, normed, inv_std, scaled, gelu_slope, hidden, branch = saved
    grid_shape = upstream.shape
    channels = grid_shape[2]
    up_float = upstream.reshape(-1, channels).astype(jnp.float32)
    grad_scale = jnp.sum(up_float * branch, axis=0)
    grad_branch = (up_float * scale_row).astype(jnp.bfloat16)
    grad_weight_out = jnp.dot(hidden.T, grad_branch, preferred_element_type=jnp.float32)
    grad_preact = (
        jnp.dot(grad_branch, weight_out_row.T, preferred_element_type=jnp.float32) * gelu_slope
    ).astype(jnp.bfloat16)
    grad_bias = jnp.sum(grad_preact.astype(jnp.float32), axis=0)
    grad_weight_in = jnp.dot(scaled.T, grad_preact, preferred_element_type=jnp.float32)
    grad_scaled = jnp.dot(grad_preact, weight_in_row.T, preferred_element_type=jnp.float32)
    grad_gain = jnp.sum(grad_scaled * normed, axis=0)
    grad_normed = grad_scaled * gain_row
    grad_conv = inv_std * (
        grad_normed
        - jnp.mean(grad_normed, axis=-1, keepdims=True)
        - normed * jnp.mean(grad_normed * normed, axis=-1, keepdims=True)
    )
    grad_conv = grad_conv.astype(jnp.bfloat16).reshape(grid_shape)
    grad_padded = extend_strip(grad_conv, strip_count)
    grad_taps = tap_sums(padded, grad_conv)
    spread = depthwise(grad_padded, kernel_taps[::-1, ::-1]).reshape(-1, channels)
    grad_field = (up_float + spread).astype(jnp.bfloat16).reshape(grid_shape)
    return (
        grad_field,
        (
            grad_taps.reshape(-1, channels),
            grad_gain,
            grad_weight_in,
            grad_bias,
            grad_weight_out,
            grad_scale,
        ),
    )


def exchanged(blocks, axis):
    return lax.all_to_all(blocks, axis, 0, 0, tiled=True)


def summed_shares(taps, gain, weight_in, bias, weight_out, scale):
    members = lax.axis_size(DP)
    layers, channels, hidden = weight_in.shape
    strips = hidden // channels
    part = channels // members
    small = jnp.concatenate(
        [
            taps.reshape(-1, channels).T,
            gain.T,
            scale.T,
            bias.reshape(layers, channels, strips).transpose(1, 0, 2).reshape(channels, -1),
        ],
        axis=1,
    )
    used = small.shape[1]
    small = jnp.pad(small, ((0, 0), (0, channels - used)))
    inward = weight_in.reshape(layers, members, part, strips, channels).transpose(1, 0, 3, 2, 4)
    outward = weight_out.reshape(layers, members, -1, channels).transpose(1, 0, 2, 3)
    rows = lax.axis_size("y")
    packed = jnp.concatenate(
        [
            small.reshape(members, rows, -1, channels),
            inward.reshape(members, rows, -1, channels),
            outward.reshape(members, rows, -1, channels),
        ],
        axis=2,
    ).astype(jnp.bfloat16)
    share = jnp.sum(exchanged(packed, DP).astype(jnp.float32), axis=0)
    piece = jnp.sum(exchanged(share.astype(jnp.bfloat16), "y").astype(jnp.float32), axis=0)
    others = lax.axis_size("zh") * lax.axis_size("c")
    copies = jnp.broadcast_to(piece.astype(jnp.bfloat16)[None], (others, *piece.shape))
    piece = jnp.sum(exchanged(copies, ("zh", "c")).astype(jnp.float32), axis=0)
    copies = jnp.broadcast_to(piece.astype(jnp.bfloat16)[None], (rows, *piece.shape))
    full = exchanged(copies, "y").astype(jnp.float32)
    first, second = part // rows, (part + layers * strips * part) // rows
    small = full[:, :first].reshape(part, channels)
    inward = full[:, first:second].reshape(layers, strips, part, channels)
    outward = full[:, second:].reshape(layers, -1, channels)
    small_t = small.T
    tap_rows = taps.shape[0] * taps.shape[1]
    return (
        small_t[:tap_rows].reshape(layers, -1, part),
        small_t[tap_rows : tap_rows + layers],
        inward.transpose(0, 2, 1, 3).reshape(layers, part, hidden),
        small[:, tap_rows + 2 * layers : used].reshape(part, layers, strips).transpose(1, 0, 2).reshape(layers, -1),
        outward,
        small_t[tap_rows + layers : tap_rows + 2 * layers],
    )


def on_device(
    fields, cotangent, face_flip, kernel, ln_gain, weight_in, bias_in, weight_out, layer_scale
):
    strip_count = lax.axis_size(TILE) // 4
    tile_index = lax.axis_index(TILE)
    height = fields.shape[1]
    width = fields.shape[2]
    channels = fields.shape[3]
    layers = kernel.shape[0]
    flipped = row_flags(face_flip, tile_index * height, height, width)
    current = orient(fields[0], flipped)
    saved_all = []
    for layer_index in range(layers):
        kernel_taps = kernel[layer_index].reshape(KS, KS, channels)
        current, saved = forward_block(
            current,
            kernel_taps,
            ln_gain[layer_index],
            weight_in[layer_index],
            bias_in[layer_index],
            weight_out[layer_index],
            layer_scale[layer_index],
            strip_count,
        )
        saved_all.append(saved)
    output = orient(current, flipped)
    grad_field = orient(cotangent[0], flipped)
    gradients = [None] * layers
    for layer_index in reversed(range(layers)):
        kernel_taps = kernel[layer_index].reshape(KS, KS, channels)
        grad_field, gradients[layer_index] = backward_block(
            grad_field,
            saved_all[layer_index],
            kernel_taps,
            ln_gain[layer_index],
            weight_in[layer_index],
            weight_out[layer_index],
            layer_scale[layer_index],
            strip_count,
        )
    normalizer = 1.0 / math.sqrt(lax.axis_size(DP) * 12 * width * width)
    shares = summed_shares(
        *(jnp.stack([entry[member] for entry in gradients]) * normalizer for member in range(6))
    )
    grad_input = orient(grad_field, flipped)
    return (
        output[None],
        grad_input[None],
        shares[0],
        shares[1],
        shares[2],
        shares[3],
        shares[4],
        shares[5],
    )


def solution(mesh):
    devices = mesh.devices
    mesh = jax.sharding.Mesh(devices.reshape(4, 8, 2, 2, 4), ("zh", "y", "c", "zl", "x"))
    return jax.shard_map(
        on_device,
        mesh=mesh,
        in_specs=(
            P(DP, TILE, None, None),
            P(DP, TILE, None, None),
            P(),
            P(),
            P(),
            P(),
            P(),
            P(),
            P(),
        ),
        out_specs=(
            P(DP, TILE, None, None),
            P(DP, TILE, None, None),
            P(None, None, DP),
            P(None, DP),
            P(None, DP, None),
            P(None, DP),
            P(None, DP, None),
            P(None, DP),
        ),
        check_vma=False,
    )
```

```python
import functools
import math

import jax
import jax.numpy as jnp
from jax import lax
from jax.experimental import pallas as pl
from jax.experimental.pallas import tpu as pltpu
from jax.sharding import PartitionSpec as P

KS = 7
TAPS = KS * KS
RIM = KS // 2
WIDE = 2 * RIM
TILE = ("zh", "y", "c")
DP = ("zl", "x")
EDGE = 16
EPSILON = 1e-06
SQRT_HALF = 0.7071067811865476
INV_ROOT_TWO_PI = 0.3989422804014327
F32 = jnp.float32
BF16 = jnp.bfloat16
GAIN_ROW = TAPS
SCALE_ROW = TAPS + 1


def dot(a, b, over=((1,), (0,))):
    return lax.dot_general(a, b, (over, ((), ())), preferred_element_type=F32)


def gelu_parts(preact):
    normal_cdf = 0.5 * (1.0 + lax.erf(preact * SQRT_HALF))
    return (
        preact * normal_cdf,
        normal_cdf + preact * jnp.exp(-0.5 * preact * preact) * INV_ROOT_TWO_PI,
    )


def picker(rows, columns, source_of):
    i = lax.broadcasted_iota(jnp.int32, (rows, columns), 0)
    j = lax.broadcasted_iota(jnp.int32, (rows, columns), 1)
    return jnp.where(j == source_of(i), 1.0, 0.0).astype(BF16)


def row_flag(flip_ref, tile_ref, row, height, width):
    place = tile_ref[0] * height + row
    column = lax.div(place, 3 * width)
    level = lax.div(lax.rem(place, 3 * width), width)
    return jnp.where(flip_ref[4 * level + column] > 0, 1, 0)


def turner(flag, width):
    return picker(width, width, lambda i: i + flag * (width - 1 - 2 * i))


def moments(convolved):
    average = jnp.mean(convolved, axis=-1, keepdims=True)
    centered = convolved - average
    inv_std = lax.rsqrt(jnp.mean(centered * centered, axis=-1, keepdims=True) + EPSILON)
    return centered * inv_std, inv_std


def tap_row(taps, t):
    return jnp.broadcast_to(taps[pl.ds(t, 1), :], (8, taps.shape[1]))


def convolve(source, width, taps, turned, rows, groups, emit):
    def group(q, carry):
        base = pl.multiple_of(q * 8, 8)
        sums = [None] * rows
        centers = [None] * rows
        for j in range(KS):
            weights = [
                tap_row(taps, TAPS - 1 - (KS * i + j) if turned else KS * i + j) for i in range(KS)
            ]
            for r in range(rows + KS - 1):
                cells = source[pl.ds(base + (r * width + j), 8), :]
                if j == RIM and 0 <= r - RIM < rows:
                    centers[r - RIM] = cells
                for i in range(KS):
                    out = r - i
                    if 0 <= out < rows:
                        term = cells * weights[i]
                        sums[out] = term if sums[out] is None else sums[out] + term
            if j == RIM:
                emit(base, centers, None)
        emit(base, None, sums)
        return carry

    lax.fori_loop(0, groups, group, 0)


def tap_sums(source, width, source_start, grad, grad_width, grad_start, rows, groups, out):
    for j in range(KS):

        def group(q, sums, j=j):
            base = pl.multiple_of(q * 8, 8)
            sums = list(sums)
            grads = [
                grad[pl.ds(base + (grad_start + r * grad_width), 8), :] for r in range(rows)
            ]
            for r in range(rows + KS - 1):
                cells = source[pl.ds(base + (source_start + r * width + j), 8), :]
                for i in range(KS):
                    if 0 <= r - i < rows:
                        sums[i] = sums[i] + cells * grads[r - i]
            return tuple(sums)

        zero = jnp.zeros((8, source.shape[1]), F32)
        sums = lax.fori_loop(0, groups, group, (zero,) * KS)
        for i in range(KS):
            out[pl.ds(KS * i + j, 1), :] = jnp.sum(sums[i], axis=0, keepdims=True)


def orient_kernel(height, width, flip, tile, fields, cotangent, canon, up, east, west):
    far = 2 * width
    to_east = picker(
        EDGE,
        far,
        lambda i: jnp.where(
            i < WIDE, width - WIDE + i, jnp.where(i < WIDE + RIM, far - RIM + i - WIDE, -1)
        ),
    )
    to_west = picker(
        EDGE, far, lambda i: jnp.where(i < WIDE, i, jnp.where(i < WIDE + RIM, width + i - WIDE, -1))
    )
    for r in range(height):
        turn = turner(row_flag(flip, tile, r, height, width), width)
        cells = slice(r * width, (r + 1) * width)
        a = dot(turn, fields[cells, :]).astype(BF16)
        b = dot(turn, cotangent[cells, :]).astype(BF16)
        canon[cells, :] = a
        up[cells, :] = b
        both = jnp.concatenate([a, b], axis=0)
        edge = slice(r * EDGE, (r + 1) * EDGE)
        east[edge, :] = dot(to_east, both).astype(BF16)
        west[edge, :] = dot(to_west, both).astype(BF16)


def widen_row(before, own, after, start, halo, width, total):
    def source_of(i):
        return jnp.where(
            i < halo,
            start + i,
            jnp.where(
                i < halo + width,
                EDGE + i - halo,
                jnp.where(i < 2 * halo + width, start + EDGE + i - halo, -1),
            ),
        )

    both = jnp.concatenate([before, own, after], axis=0)
    return dot(picker(total, width + 2 * EDGE, source_of), both).astype(BF16)


def widen_kernel(height, width, before, after, canon, up, canon_x, up_x, to_next, to_prev):
    full, slim = width + 16, width + 8
    for r in range(height):
        edge = slice(r * EDGE, (r + 1) * EDGE)
        cells = slice(r * width, (r + 1) * width)
        a = widen_row(before[edge, :], canon[cells, :], after[edge, :], 0, WIDE, width, full)
        b = widen_row(before[edge, :], up[cells, :], after[edge, :], WIDE, RIM, width, slim)
        canon_x[r * full : (r + 1) * full, :] = a
        up_x[r * slim : (r + 1) * slim, :] = b
        if r < WIDE:
            to_prev[r * full : (r + 1) * full, :] = a
        if r < RIM:
            to_prev[WIDE * full + r * slim : WIDE * full + (r + 1) * slim, :] = b
        if r >= height - WIDE:
            k = r - (height - WIDE)
            to_next[k * full : (k + 1) * full, :] = a
        if r >= height - RIM:
            k = r - (height - RIM)
            to_next[WIDE * full + k * slim : WIDE * full + (k + 1) * slim, :] = b


def widen_grad_kernel(height, width, before, after, grad, grad_x, to_next, to_prev):
    full = width + 16
    for r in range(height):
        edge = slice(r * EDGE, (r + 1) * EDGE)
        cells = slice(r * width, (r + 1) * width)
        a = widen_row(before[edge, :], grad[cells, :], after[edge, :], 0, WIDE, width, full)
        grad_x[r * full : (r + 1) * full, :] = a
        if r < WIDE:
            to_prev[r * full : (r + 1) * full, :] = a
        if r >= height - WIDE:
            k = r - (height - WIDE)
            to_next[k * full : (k + 1) * full, :] = a


def join_rows(target, above, middle, below, count, start):
    rows = middle.shape[0]
    target[0:count, :] = above[start : start + count, :].astype(F32)
    target[count : count + rows, :] = middle[...].astype(F32)
    target[count + rows : 2 * count + rows, :] = below[start : start + count, :].astype(F32)


def forward_kernel(
    height,
    width,
    flip,
    tile,
    above,
    canon_x,
    below,
    up,
    kernel,
    gain,
    weight_in,
    bias,
    weight_out,
    scale,
    result,
    conv0,
    slope0,
    hidden0,
    h1,
    grad_conv,
    east,
    west,
    big,
    bias_sum,
    rows_out,
    x_scratch,
    taps,
    h1_flat,
    middle,
    conv1,
    in_sum,
    out_sum,
):
    full, slim = width + 16, width + 8
    rim_rows = height + 2 * RIM
    join_rows(x_scratch, above, canon_x, below, WIDE * full, 0)
    taps[0:TAPS, :] = kernel[0].astype(F32)

    def emit0(base, centers, sums):
        for r in range(rim_rows):
            if centers is not None:
                h1_flat[pl.ds(base + r * slim, 8), :] = centers[r]
            else:
                conv0[pl.ds(base + r * slim, 8), :] = sums[r]

    convolve(x_scratch, full, taps, False, rim_rows, slim // 8, emit0)

    chunk0 = 2 * slim

    def block0(k, carry):
        cells = pl.ds(pl.multiple_of(k * chunk0, 16), chunk0)
        normed, _ = moments(conv0[cells, :])
        scaled = (normed * gain[0:1, :]).astype(BF16)
        preact = dot(scaled, weight_in[0]) + bias[0:1, :]
        value, slope = gelu_parts(preact)
        hidden = value.astype(BF16)
        slope0[cells, :] = slope.astype(BF16)
        hidden0[cells, :] = hidden
        branch = dot(hidden, weight_out[0])
        state = (h1_flat[cells, :] + scale[0:1, :] * branch).astype(BF16)
        h1[cells, :] = state
        h1_flat[cells, :] = state.astype(F32)
        return carry

    lax.fori_loop(0, rim_rows // 2, block0, 0)

    taps[0:TAPS, :] = kernel[1].astype(F32)

    def emit1(base, centers, sums):
        for r in range(height):
            if centers is not None:
                middle[pl.ds(base + r * width, 8), :] = centers[r]
            else:
                conv1[pl.ds(base + r * width, 8), :] = sums[r]

    convolve(h1_flat, slim, taps, False, height, width // 8, emit1)

    in_sum[...] = jnp.zeros_like(in_sum)
    out_sum[...] = jnp.zeros_like(out_sum)
    bias_sum[...] = jnp.zeros_like(bias_sum)
    rows_out[...] = jnp.zeros_like(rows_out)
    chunk_rows = 3
    chunk1 = chunk_rows * width
    ones = jnp.ones((8, chunk1), BF16)
    to_east = picker(EDGE, width, lambda i: jnp.where(i < WIDE, width - WIDE + i, -1))
    to_west = picker(EDGE, width, lambda i: jnp.where(i < WIDE, i, -1))

    def block1(k, carry):
        cells = pl.ds(pl.multiple_of(k * chunk1, 8), chunk1)
        normed, inv_std = moments(conv1[cells, :])
        gain_row = gain[1:2, :]
        scaled = (normed * gain_row).astype(BF16)
        preact = dot(scaled, weight_in[1]) + bias[1:2, :]
        value, slope = gelu_parts(preact)
        hidden = value.astype(BF16)
        branch = dot(hidden, weight_out[1])
        scale_row = scale[1:2, :]
        state = (middle[cells, :] + scale_row * branch).astype(BF16)
        upstream = up[cells, :]
        grad_branch = (upstream.astype(F32) * scale_row).astype(BF16)
        out_sum[...] += dot(upstream, hidden, ((0,), (0,)))
        grad_preact = (dot(grad_branch, weight_out[1], ((1,), (1,))) * slope).astype(BF16)
        bias_sum[...] += dot(ones, grad_preact)
        in_sum[...] += dot(scaled, grad_preact, ((0,), (0,)))
        grad_scaled = dot(grad_preact, weight_in[1], ((1,), (1,)))
        rows_out[GAIN_ROW : GAIN_ROW + 1, :] += jnp.sum(
            grad_scaled * normed, axis=0, keepdims=True
        )
        e = grad_scaled * gain_row
        grad = inv_std * (
            e
            - jnp.mean(e, axis=-1, keepdims=True)
            - normed * jnp.mean(e * normed, axis=-1, keepdims=True)
        )
        grad = grad.astype(BF16)
        grad_conv[cells, :] = grad
        for r in range(chunk_rows):
            row = k * chunk_rows + r
            turn = turner(row_flag(flip, tile, row, height, width), width)
            own = slice(r * width, (r + 1) * width)
            result[pl.ds(pl.multiple_of(row * width, 8), width), :] = dot(turn, state[own]).astype(
                BF16
            )
            edge = pl.ds(pl.multiple_of(row * EDGE, 8), EDGE)
            east[edge, :] = dot(to_east, grad[own]).astype(BF16)
            west[edge, :] = dot(to_west, grad[own]).astype(BF16)
        return carry

    lax.fori_loop(0, height // chunk_rows, block1, 0)
    pack_weights(in_sum, out_sum, weight_out[1], scale[1:2, :], big, 0, rows_out)


def pack_weights(in_sum, out_sum, weight_out, scale_row, big, first, rows_out):
    channels = in_sum.shape[0]
    members = big.shape[0]
    part = channels // members
    products = out_sum[...].T
    rows_out[SCALE_ROW : SCALE_ROW + 1, :] = jnp.sum(
        products * weight_out.astype(F32), axis=0, keepdims=True
    )
    outward = products * scale_row
    strips = in_sum.shape[1] // channels
    share = outward.shape[0] // members
    piece = share // strips
    for d in range(members):
        for s in range(strips):
            big[d, first + s, 0:part, :] = in_sum[
                d * part : (d + 1) * part, s * channels : (s + 1) * channels
            ].astype(BF16)
            begin = d * share + s * piece
            big[d, first + s, part : part + piece, :] = outward[begin : begin + piece, :].astype(
                BF16
            )


def taps_kernel(height, width, h1, grad_conv, out, source, grad):
    slim = width + 8
    source[...] = h1[...].astype(F32)
    grad[...] = grad_conv[...].astype(F32)
    tap_sums(source, slim, 0, grad, width, 0, height, width // 8, out)


def backward_kernel(
    height,
    width,
    flip,
    tile,
    above,
    grad_x,
    below,
    x_above,
    canon_x,
    x_below,
    up_x,
    kernel,
    gain,
    weight_in,
    weight_out,
    scale,
    conv0,
    slope0,
    hidden0,
    big1,
    bias1,
    rows1,
    taps1,
    grad_input,
    packed,
    g_scratch,
    taps,
    up_flat,
    d_flat,
    g0_flat,
    in_sum,
    out_sum,
    bias_sum,
    rows_all,
):
    full, slim = width + 16, width + 8
    rim_rows = height + 2 * RIM
    channels = gain.shape[1]
    join_rows(g_scratch, above, grad_x, below, WIDE * full, 0)
    join_rows(up_flat, x_above, up_x, x_below, RIM * slim, WIDE * full)
    taps[0:TAPS, :] = kernel[1].astype(F32)

    def emit1(base, centers, sums):
        if sums is not None:
            for r in range(rim_rows):
                cells = pl.ds(base + r * slim, 8)
                d_flat[cells, :] = (up_flat[cells, :] + sums[r]).astype(BF16).astype(F32)

    convolve(g_scratch, full, taps, True, rim_rows, slim // 8, emit1)

    in_sum[...] = jnp.zeros_like(in_sum)
    out_sum[...] = jnp.zeros_like(out_sum)
    bias_sum[...] = jnp.zeros_like(bias_sum)
    rows_all[...] = jnp.zeros_like(rows_all)
    half = rows1.shape[0]
    chunk = 2 * slim

    def owned(k, shape, dim):
        place = lax.broadcasted_iota(jnp.int32, shape, dim)
        second = jnp.where(place >= slim, 1, 0)
        row = 2 * k + second
        column = place - slim * second
        inside = (
            (row >= RIM) & (row < RIM + height) & (column >= RIM) & (column < RIM + width)
        )
        return jnp.where(inside, 1.0, 0.0)

    def block0(k, carry):
        cells = pl.ds(pl.multiple_of(k * chunk, 16), chunk)
        mask = owned(k, (chunk, channels), 0)
        normed, inv_std = moments(conv0[cells, :])
        gain_row = gain[0:1, :]
        scaled = (normed * gain_row * mask).astype(BF16)
        upstream = d_flat[cells, :]
        grad_branch = (upstream * scale[0:1, :]).astype(BF16)
        out_sum[...] += dot((upstream * mask).astype(BF16), hidden0[cells, :], ((0,), (0,)))
        grad_preact = (
            dot(grad_branch, weight_out[0], ((1,), (1,))) * slope0[cells, :].astype(F32)
        ).astype(BF16)
        bias_sum[...] += dot(owned(k, (8, chunk), 1).astype(BF16), grad_preact)
        in_sum[...] += dot(scaled, grad_preact, ((0,), (0,)))
        grad_scaled = dot(grad_preact, weight_in[0], ((1,), (1,)))
        rows_all[GAIN_ROW : GAIN_ROW + 1, :] += jnp.sum(
            grad_scaled * normed * mask, axis=0, keepdims=True
        )
        e = grad_scaled * gain_row
        grad = inv_std * (
            e
            - jnp.mean(e, axis=-1, keepdims=True)
            - normed * jnp.mean(e * normed, axis=-1, keepdims=True)
        )
        g0_flat[cells, :] = grad.astype(BF16).astype(F32)
        return carry

    lax.fori_loop(0, rim_rows // 2, block0, 0)

    taps[0:TAPS, :] = kernel[0].astype(F32)

    def emit0(base, centers, sums):
        if sums is not None:
            for r in range(height):
                own = d_flat[pl.ds(base + ((r + RIM) * slim + RIM), 8), :]
                up_flat[pl.ds(base + r * width, 8), :] = own + sums[r]

    convolve(g0_flat, slim, taps, True, height, width // 8, emit0)
    for r in range(height):
        turn = turner(row_flag(flip, tile, r, height, width), width)
        cells = slice(r * width, (r + 1) * width)
        grad_input[cells, :] = dot(turn, up_flat[cells, :].astype(BF16)).astype(BF16)

    join_rows(g_scratch, x_above, canon_x, x_below, WIDE * full, 0)
    tap_sums(
        g_scratch,
        full,
        RIM * full + RIM,
        g0_flat,
        slim,
        RIM * slim + RIM,
        height,
        width // 8,
        rows_all,
    )
    strips = big1.shape[1]
    pack_weights(in_sum, out_sum, weight_out[0], scale[0:1, :], packed, 0, rows_all)
    big_rows = big1.shape[2]
    packed[:, strips:, 0:big_rows, :] = big1[...]
    rows_all[half:, :] = rows1[...]
    rows_all[half : half + TAPS, :] = taps1[0:TAPS, :]
    small = rows_all[...].T
    members = packed.shape[0]
    part = channels // members
    zeros = jnp.zeros((8, channels), BF16)
    for d in range(members):
        for y in range(2 * strips):
            if y < part // 8:
                begin = d * part + 8 * y
                rows = small[begin : begin + 8, :].astype(BF16)
            elif y < part // 8 + 2:
                sums = bias_sum if y == part // 8 else bias1
                lane = (d // 2) * channels
                rows = sums[:, lane : lane + channels]
                if d % 2:
                    rows = pltpu.roll(rows, channels // 2, 1)
                rows = rows.astype(BF16)
            else:
                rows = zeros
            packed[d, y, big_rows : big_rows + 8, :] = rows


def shape_of(*sizes, dtype=BF16):
    return jax.ShapeDtypeStruct(sizes, dtype)


def call(body, outs, flags=0, ins=0, scratch=(), cost=None):
    smem = pl.BlockSpec(memory_space=pltpu.SMEM)
    vmem = pl.BlockSpec(memory_space=pltpu.VMEM)
    return pl.pallas_call(
        body,
        out_shape=outs,
        in_specs=[smem] * flags + [vmem] * ins,
        out_specs=[vmem] * len(outs),
        scratch_shapes=[pltpu.VMEM(s, F32) for s in scratch],
        cost_estimate=cost,
    )


def shifted(block, axis, distance):
    count = lax.axis_size(axis)
    return lax.ppermute(block, axis, [(i, (i + distance) % count) for i in range(count)])


def exchanged(blocks, axis):
    return lax.all_to_all(blocks, axis, 0, 0, tiled=True)


def summed_shares(packed, hidden):
    members, rows, _, channels = packed.shape
    part = channels // members
    layers = 2
    strips = rows // layers
    share = jnp.sum(exchanged(packed, DP).astype(F32), axis=0)
    piece = jnp.sum(exchanged(share.astype(BF16), "y").astype(F32), axis=0)
    others = lax.axis_size("zh") * lax.axis_size("c")
    copies = jnp.broadcast_to(piece.astype(BF16)[None], (others, *piece.shape))
    piece = jnp.sum(exchanged(copies, ("zh", "c")).astype(F32), axis=0)
    copies = jnp.broadcast_to(piece.astype(BF16)[None], (rows, *piece.shape))
    return exchanged(copies, "y")


def unpacked(full, normalizer, hidden, members):
    rows, _, channels = full.shape
    layers = 2
    strips = rows // layers
    part = channels // members
    piece = hidden // members // strips
    full = full.astype(F32) * normalizer
    inward = full[:, :part].reshape(layers, strips, part, channels)
    outward = full[:, part : part + piece].reshape(layers, -1, channels)
    rest = full[:, part + piece :]
    small = rest[: part // 8].reshape(part, layers, channels // layers).transpose(1, 2, 0)
    bias = rest[part // 8 : part // 8 + layers, 0, : hidden // members]
    return (
        small[:, :TAPS],
        small[:, GAIN_ROW],
        inward.transpose(0, 2, 1, 3).reshape(layers, part, hidden),
        bias,
        outward,
        small[:, SCALE_ROW],
    )


def on_device(
    fields, cotangent, face_flip, kernel, ln_gain, weight_in, bias_in, weight_out, layer_scale
):
    height, width, channels = fields.shape[1:]
    hidden = weight_in.shape[2]
    members = lax.axis_size(DP)
    own, full, slim = height * width, width + 16, width + 8
    rim_rows = height + 2 * RIM
    rim = rim_rows * slim
    tall = (height + 2 * WIDE) * full
    sent = WIDE * full + RIM * slim
    strips = hidden // channels
    big_rows = channels // members + hidden // members // strips
    tile = lax.axis_index(TILE).astype(jnp.int32).reshape(1)

    cells = shape_of(own, channels)
    edges = shape_of(height * EDGE, channels)
    canon, up, east, west = call(
        functools.partial(orient_kernel, height, width), [cells, cells, edges, edges], 2, 2
    )(face_flip, tile, fields.reshape(own, channels), cotangent.reshape(own, channels))
    before = shifted(east, "zh", 1)
    after = shifted(west, "zh", -1)
    canon_x, up_x, to_next, to_prev = call(
        functools.partial(widen_kernel, height, width),
        [
            shape_of(height * full, channels),
            shape_of(height * slim, channels),
            shape_of(sent, channels),
            shape_of(sent, channels),
        ],
        0,
        4,
    )(before, after, canon, up)
    above = shifted(to_next, TILE, 1)
    below = shifted(to_prev, TILE, -1)
    sums = (channels, hidden)
    (
        result,
        conv0,
        slope0,
        hidden0,
        h1,
        grad_conv,
        east,
        west,
        big1,
        bias1,
        rows1,
    ) = call(
        functools.partial(forward_kernel, height, width),
        [
            cells,
            shape_of(rim, channels, dtype=F32),
            shape_of(rim, hidden),
            shape_of(rim, hidden),
            shape_of(rim, channels),
            cells,
            edges,
            edges,
            shape_of(members, strips, big_rows, channels),
            shape_of(8, hidden, dtype=F32),
            shape_of(64, channels, dtype=F32),
        ],
        2,
        10,
        [
            (tall, channels),
            (56, channels),
            (rim, channels),
            (own, channels),
            (own, channels),
            sums,
            sums,
        ],
    )(
        face_flip,
        tile,
        above,
        canon_x,
        below,
        up,
        kernel,
        ln_gain,
        weight_in,
        bias_in,
        weight_out,
        layer_scale,
    )
    before = shifted(east, "zh", 1)
    after = shifted(west, "zh", -1)
    (taps1,) = call(
        functools.partial(taps_kernel, height, width),
        [shape_of(56, channels, dtype=F32)],
        0,
        2,
        [(rim, channels), (own, channels)],
        pl.CostEstimate(flops=2 * TAPS * own * channels, bytes_accessed=1 << 20, transcendentals=0),
    )(h1, grad_conv)
    grad_x, to_next, to_prev = call(
        functools.partial(widen_grad_kernel, height, width),
        [
            shape_of(height * full, channels),
            shape_of(WIDE * full, channels),
            shape_of(WIDE * full, channels),
        ],
        0,
        3,
    )(before, after, grad_conv)
    grad_above = shifted(to_next, TILE, 1)
    grad_below = shifted(to_prev, TILE, -1)
    grad_input, packed = call(
        functools.partial(backward_kernel, height, width),
        [cells, shape_of(members, 2 * strips, big_rows + 8, channels)],
        2,
        19,
        [
            (tall, channels),
            (56, channels),
            (rim, channels),
            (rim, channels),
            (rim, channels),
            sums,
            sums,
            (8, hidden),
            (128, channels),
        ],
    )(
        face_flip,
        tile,
        grad_above,
        grad_x,
        grad_below,
        above,
        canon_x,
        below,
        up_x,
        kernel,
        ln_gain,
        weight_in,
        weight_out,
        layer_scale,
        conv0,
        slope0,
        hidden0,
        big1,
        bias1,
        rows1,
        taps1,
    )
    normalizer = 1.0 / math.sqrt(members * 12 * width * width)
    shares = unpacked(summed_shares(packed, hidden), normalizer, hidden, members)
    return (result.reshape(fields.shape), grad_input.reshape(fields.shape), *shares)


def solution(mesh, sizes=(4, 8, 2, 2, 4)):
    mesh = jax.sharding.Mesh(mesh.devices.reshape(sizes), ("zh", "y", "c", "zl", "x"))
    return jax.shard_map(
        on_device,
        mesh=mesh,
        in_specs=(P(DP, TILE, None, None), P(DP, TILE, None, None)) + (P(),) * 7,
        out_specs=(
            P(DP, TILE, None, None),
            P(DP, TILE, None, None),
            P(None, None, DP),
            P(None, DP),
            P(None, DP, None),
            P(None, DP),
            P(None, DP, None),
            P(None, DP),
        ),
        check_vma=False,
    )
```

```python
import functools
import math

import jax
import jax.numpy as jnp
from jax import lax
from jax.experimental import pallas as pl
from jax.experimental.pallas import tpu as pltpu
from jax.sharding import PartitionSpec as P

KS = 7
TAPS = KS * KS
RIM = KS // 2
WIDE = 2 * RIM
TILE = ("zh", "y", "c")
DP = ("zl", "x")
EDGE = 16
LIMIT = 24 << 20
EPSILON = 1e-06
SQRT_HALF = 0.7071067811865476
INV_ROOT_TWO_PI = 0.3989422804014327
F32 = jnp.float32
BF16 = jnp.bfloat16
GAIN_ROW = TAPS
SCALE_ROW = TAPS + 1


def dot(a, b, over=((1,), (0,))):
    return lax.dot_general(a, b, (over, ((), ())), preferred_element_type=F32)


def gelu_parts(preact):
    normal_cdf = 0.5 * (1.0 + lax.erf(preact * SQRT_HALF))
    return (
        preact * normal_cdf,
        normal_cdf + preact * jnp.exp(-0.5 * preact * preact) * INV_ROOT_TWO_PI,
    )


def picker(rows, columns, source_of):
    i = lax.broadcasted_iota(jnp.int32, (rows, columns), 0)
    j = lax.broadcasted_iota(jnp.int32, (rows, columns), 1)
    return jnp.where(j == source_of(i), 1.0, 0.0).astype(BF16)


def row_flag(flip_ref, tile_ref, row, height, width):
    place = tile_ref[0] * height + row
    column = lax.div(place, 3 * width)
    level = lax.div(lax.rem(place, 3 * width), width)
    return jnp.where(flip_ref[4 * level + column] > 0, 1, 0)


def turner(flag, width):
    return picker(width, width, lambda i: i + flag * (width - 1 - 2 * i))


def moments(convolved):
    average = jnp.mean(convolved, axis=-1, keepdims=True)
    centered = convolved - average
    inv_std = lax.rsqrt(jnp.mean(centered * centered, axis=-1, keepdims=True) + EPSILON)
    return centered * inv_std, inv_std


def tap_row(taps, t):
    return jnp.broadcast_to(taps[pl.ds(t, 1), :], (8, taps.shape[1]))


def convolve(source, width, taps, turned, rows, groups, emit):
    def group(q, carry):
        base = pl.multiple_of(q * 8, 8)
        sums = [None] * rows
        centers = [None] * rows
        for j in range(KS):
            weights = [
                tap_row(taps, TAPS - 1 - (KS * i + j) if turned else KS * i + j) for i in range(KS)
            ]
            for r in range(rows + KS - 1):
                cells = source[pl.ds(base + (r * width + j), 8), :]
                if j == RIM and 0 <= r - RIM < rows:
                    centers[r - RIM] = cells
                for i in range(KS):
                    out = r - i
                    if 0 <= out < rows:
                        term = cells * weights[i]
                        sums[out] = term if sums[out] is None else sums[out] + term
            if j == RIM:
                emit(base, centers, None)
        emit(base, None, sums)
        return carry

    lax.fori_loop(0, groups, group, 0)


def tap_sums(source, width, source_start, grad, grad_width, grad_start, rows, groups, out):
    for j in range(KS):

        def group(q, sums, j=j):
            base = pl.multiple_of(q * 8, 8)
            sums = list(sums)
            grads = [
                grad[pl.ds(base + (grad_start + r * grad_width), 8), :] for r in range(rows)
            ]
            for r in range(rows + KS - 1):
                cells = source[pl.ds(base + (source_start + r * width + j), 8), :]
                for i in range(KS):
                    if 0 <= r - i < rows:
                        sums[i] = sums[i] + cells * grads[r - i]
            return tuple(sums)

        zero = jnp.zeros((8, source.shape[1]), F32)
        sums = lax.fori_loop(0, groups, group, (zero,) * KS)
        for i in range(KS):
            out[pl.ds(KS * i + j, 1), :] = jnp.sum(sums[i], axis=0, keepdims=True)


def edge_kernel(height, width, flip, tile, fields, cotangent, east, west):
    far = 2 * width

    def turned(flag, i):
        return jnp.where(
            i >= width, width + i - width + flag * (3 * width - 1 - 2 * i), i + flag * (width - 1 - 2 * i)
        )

    def east_of(flag, i):
        place = jnp.where(i < WIDE, width - WIDE + i, far - RIM + i - WIDE)
        return jnp.where(i < WIDE + RIM, turned(flag, place), -1)

    def west_of(flag, i):
        place = jnp.where(i < WIDE, i, width + i - WIDE)
        return jnp.where(i < WIDE + RIM, turned(flag, place), -1)

    picks = []
    for flag in (0, 1):
        to_east = picker(EDGE, far, functools.partial(east_of, flag)).astype(F32)
        to_west = picker(EDGE, far, functools.partial(west_of, flag)).astype(F32)
        picks.append(jnp.concatenate([to_east, to_west], axis=0))
    for r in range(height):
        flag = row_flag(flip, tile, r, height, width)
        cells = slice(r * width, (r + 1) * width)
        both = jnp.concatenate([fields[cells, :], cotangent[cells, :]], axis=0)
        pick = jnp.where(flag > 0, picks[1], picks[0]).astype(BF16)
        edges = dot(pick, both).astype(BF16)
        edge = slice(r * EDGE, (r + 1) * EDGE)
        east[edge, :] = edges[:EDGE]
        west[edge, :] = edges[EDGE:]


def orient_kernel(height, width, flip, tile, fields, cotangent, canon, up):
    plain = turner(0, width).astype(F32)
    flipped = turner(1, width).astype(F32)
    for r in range(height):
        flag = row_flag(flip, tile, r, height, width)
        turn = jnp.where(flag > 0, flipped, plain).astype(BF16)
        cells = slice(r * width, (r + 1) * width)
        canon[cells, :] = dot(turn, fields[cells, :]).astype(BF16)
        up[cells, :] = dot(turn, cotangent[cells, :]).astype(BF16)


def widen_row(before, own, after, start, halo, width, total):
    def source_of(i):
        return jnp.where(
            i < halo,
            start + i,
            jnp.where(
                i < halo + width,
                EDGE + i - halo,
                jnp.where(i < 2 * halo + width, start + EDGE + i - halo, -1),
            ),
        )

    both = jnp.concatenate([before, own, after], axis=0)
    return dot(picker(total, width + 2 * EDGE, source_of), both).astype(BF16)


def widen_kernel(height, width, before, after, canon, up, canon_x, up_x, to_next, to_prev):
    full, slim = width + 16, width + 8
    for r in range(height):
        edge = slice(r * EDGE, (r + 1) * EDGE)
        cells = slice(r * width, (r + 1) * width)
        a = widen_row(before[edge, :], canon[cells, :], after[edge, :], 0, WIDE, width, full)
        b = widen_row(before[edge, :], up[cells, :], after[edge, :], WIDE, RIM, width, slim)
        canon_x[r * full : (r + 1) * full, :] = a
        up_x[r * slim : (r + 1) * slim, :] = b
        if r < WIDE:
            to_prev[r * full : (r + 1) * full, :] = a
        if r < RIM:
            to_prev[WIDE * full + r * slim : WIDE * full + (r + 1) * slim, :] = b
        if r >= height - WIDE:
            k = r - (height - WIDE)
            to_next[k * full : (k + 1) * full, :] = a
        if r >= height - RIM:
            k = r - (height - RIM)
            to_next[WIDE * full + k * slim : WIDE * full + (k + 1) * slim, :] = b


def widen_grad_kernel(height, width, before, after, grad, grad_x, to_next, to_prev):
    full = width + 16
    for r in range(height):
        edge = slice(r * EDGE, (r + 1) * EDGE)
        cells = slice(r * width, (r + 1) * width)
        a = widen_row(before[edge, :], grad[cells, :], after[edge, :], 0, WIDE, width, full)
        grad_x[r * full : (r + 1) * full, :] = a
        if r < WIDE:
            to_prev[r * full : (r + 1) * full, :] = a
        if r >= height - WIDE:
            k = r - (height - WIDE)
            to_next[k * full : (k + 1) * full, :] = a


def join_rows(target, above, middle, below, count, start):
    rows = middle.shape[0]
    target[0:count, :] = above[start : start + count, :].astype(F32)
    target[count : count + rows, :] = middle[...].astype(F32)
    target[count + rows : 2 * count + rows, :] = below[start : start + count, :].astype(F32)


def forward_kernel(
    height,
    width,
    flip,
    tile,
    above,
    canon_x,
    below,
    up,
    kernel,
    gain,
    weight_in,
    bias,
    weight_out,
    scale,
    result,
    conv0,
    slope0,
    hidden0,
    h1,
    grad_conv,
    east,
    west,
    scaled1,
    hidden1,
    grad_preact1,
    gain_sum,
    x_scratch,
    taps,
    h1_flat,
    middle,
    conv1,
):
    full, slim = width + 16, width + 8
    rim_rows = height + 2 * RIM
    join_rows(x_scratch, above, canon_x, below, WIDE * full, 0)
    taps[0:TAPS, :] = kernel[0].astype(F32)

    def emit0(base, centers, sums):
        for r in range(rim_rows):
            if centers is not None:
                h1_flat[pl.ds(base + r * slim, 8), :] = centers[r]
            else:
                conv0[pl.ds(base + r * slim, 8), :] = sums[r]

    convolve(x_scratch, full, taps, False, rim_rows, slim // 8, emit0)

    chunk0 = 2 * slim

    def block0(k, carry):
        cells = pl.ds(pl.multiple_of(k * chunk0, 16), chunk0)
        normed, _ = moments(conv0[cells, :])
        scaled = (normed * gain[0:1, :]).astype(BF16)
        preact = dot(scaled, weight_in[0]) + bias[0:1, :]
        value, slope = gelu_parts(preact)
        hidden = value.astype(BF16)
        slope0[cells, :] = slope.astype(BF16)
        hidden0[cells, :] = hidden
        branch = dot(hidden, weight_out[0])
        state = (h1_flat[cells, :] + scale[0:1, :] * branch).astype(BF16)
        h1[cells, :] = state
        h1_flat[cells, :] = state.astype(F32)
        return carry

    lax.fori_loop(0, rim_rows // 2, block0, 0)

    taps[0:TAPS, :] = kernel[1].astype(F32)

    def emit1(base, centers, sums):
        for r in range(height):
            if centers is not None:
                middle[pl.ds(base + r * width, 8), :] = centers[r]
            else:
                conv1[pl.ds(base + r * width, 8), :] = sums[r]

    convolve(h1_flat, slim, taps, False, height, width // 8, emit1)

    gain_sum[...] = jnp.zeros_like(gain_sum)
    chunk_rows = 3
    chunk1 = chunk_rows * width
    to_east = picker(EDGE, width, lambda i: jnp.where(i < WIDE, width - WIDE + i, -1))
    to_west = picker(EDGE, width, lambda i: jnp.where(i < WIDE, i, -1))

    def block1(k, carry):
        cells = pl.ds(pl.multiple_of(k * chunk1, 8), chunk1)
        normed, inv_std = moments(conv1[cells, :])
        gain_row = gain[1:2, :]
        scaled = (normed * gain_row).astype(BF16)
        preact = dot(scaled, weight_in[1]) + bias[1:2, :]
        value, slope = gelu_parts(preact)
        hidden = value.astype(BF16)
        branch = dot(hidden, weight_out[1])
        scale_row = scale[1:2, :]
        state = (middle[cells, :] + scale_row * branch).astype(BF16)
        upstream = up[cells, :]
        grad_branch = (upstream.astype(F32) * scale_row).astype(BF16)
        grad_preact = (dot(grad_branch, weight_out[1], ((1,), (1,))) * slope).astype(BF16)
        scaled1[cells, :] = scaled
        hidden1[cells, :] = hidden
        grad_preact1[cells, :] = grad_preact
        grad_scaled = dot(grad_preact, weight_in[1], ((1,), (1,)))
        gain_sum[0:1, :] += jnp.sum(
            grad_scaled * normed, axis=0, keepdims=True
        )
        e = grad_scaled * gain_row
        grad = inv_std * (
            e
            - jnp.mean(e, axis=-1, keepdims=True)
            - normed * jnp.mean(e * normed, axis=-1, keepdims=True)
        )
        grad = grad.astype(BF16)
        grad_conv[cells, :] = grad
        for r in range(chunk_rows):
            row = k * chunk_rows + r
            turn = turner(row_flag(flip, tile, row, height, width), width)
            own = slice(r * width, (r + 1) * width)
            result[pl.ds(pl.multiple_of(row * width, 8), width), :] = dot(turn, state[own]).astype(
                BF16
            )
            edge = pl.ds(pl.multiple_of(row * EDGE, 8), EDGE)
            east[edge, :] = dot(to_east, grad[own]).astype(BF16)
            west[edge, :] = dot(to_west, grad[own]).astype(BF16)
        return carry

    lax.fori_loop(0, height // chunk_rows, block1, 0)


def weights_kernel(
    scaled, hidden, grad_preact, up, gain_sum, weight_out, scale, big, bias_sum, rows_out, in_sum, out_sum
):
    in_sum[...] = jnp.zeros_like(in_sum)
    out_sum[...] = jnp.zeros_like(out_sum)
    bias_sum[...] = jnp.zeros_like(bias_sum)
    rows_out[...] = jnp.zeros_like(rows_out)
    steps = 3
    chunk = scaled.shape[0] // steps
    ones = jnp.ones((8, chunk), BF16)

    def step(k, carry):
        cells = pl.ds(pl.multiple_of(k * chunk, 8), chunk)
        out_sum[...] += dot(up[cells, :], hidden[cells, :], ((0,), (0,)))
        bias_sum[...] += dot(ones, grad_preact[cells, :])
        in_sum[...] += dot(scaled[cells, :], grad_preact[cells, :], ((0,), (0,)))
        return carry

    lax.fori_loop(0, steps, step, 0)
    rows_out[GAIN_ROW : GAIN_ROW + 1, :] = gain_sum[0:1, :]
    pack_weights(in_sum, out_sum, weight_out[1], scale[1:2, :], big, 0, rows_out)


def pack_weights(in_sum, out_sum, weight_out, scale_row, big, first, rows_out):
    channels = in_sum.shape[0]
    members = big.shape[0]
    part = channels // members
    products = out_sum[...].T
    rows_out[SCALE_ROW : SCALE_ROW + 1, :] = jnp.sum(
        products * weight_out.astype(F32), axis=0, keepdims=True
    )
    outward = products * scale_row
    strips = in_sum.shape[1] // channels
    share = outward.shape[0] // members
    piece = share // strips
    for d in range(members):
        for s in range(strips):
            big[d, first + s, 0:part, :] = in_sum[
                d * part : (d + 1) * part, s * channels : (s + 1) * channels
            ].astype(BF16)
            begin = d * share + s * piece
            big[d, first + s, part : part + piece, :] = outward[begin : begin + piece, :].astype(
                BF16
            )


def taps_kernel(height, width, h1, grad_conv, out, source, grad):
    slim = width + 8
    source[...] = h1[...].astype(F32)
    grad[...] = grad_conv[...].astype(F32)
    tap_sums(source, slim, 0, grad, width, 0, height, width // 8, out)


def backward_kernel(
    height,
    width,
    above,
    grad_x,
    below,
    x_above,
    canon_x,
    x_below,
    up_x,
    kernel,
    gain,
    weight_in,
    weight_out,
    scale,
    conv0,
    slope0,
    hidden0,
    big1,
    bias1,
    rows1,
    taps1,
    d1,
    grad0,
    packed,
    g_scratch,
    taps,
    up_flat,
    d_flat,
    g0_flat,
    in_sum,
    out_sum,
    bias_sum,
    rows_all,
):
    full, slim = width + 16, width + 8
    rim_rows = height + 2 * RIM
    channels = gain.shape[1]
    join_rows(g_scratch, above, grad_x, below, WIDE * full, 0)
    join_rows(up_flat, x_above, up_x, x_below, RIM * slim, WIDE * full)
    taps[0:TAPS, :] = kernel[1].astype(F32)

    def emit1(base, centers, sums):
        if sums is not None:
            for r in range(rim_rows):
                cells = pl.ds(base + r * slim, 8)
                d_flat[cells, :] = (up_flat[cells, :] + sums[r]).astype(BF16).astype(F32)

    convolve(g_scratch, full, taps, True, rim_rows, slim // 8, emit1)

    in_sum[...] = jnp.zeros_like(in_sum)
    out_sum[...] = jnp.zeros_like(out_sum)
    bias_sum[...] = jnp.zeros_like(bias_sum)
    rows_all[...] = jnp.zeros_like(rows_all)
    half = rows1.shape[0]
    chunk = 2 * slim

    def owned(k, shape, dim):
        place = lax.broadcasted_iota(jnp.int32, shape, dim)
        second = jnp.where(place >= slim, 1, 0)
        row = 2 * k + second
        column = place - slim * second
        inside = (
            (row >= RIM) & (row < RIM + height) & (column >= RIM) & (column < RIM + width)
        )
        return jnp.where(inside, 1.0, 0.0)

    def block0(k, carry):
        cells = pl.ds(pl.multiple_of(k * chunk, 16), chunk)
        mask = owned(k, (chunk, channels), 0)
        normed, inv_std = moments(conv0[cells, :])
        gain_row = gain[0:1, :]
        scaled = (normed * gain_row * mask).astype(BF16)
        upstream = d_flat[cells, :]
        grad_branch = (upstream * scale[0:1, :]).astype(BF16)
        out_sum[...] += dot((upstream * mask).astype(BF16), hidden0[cells, :], ((0,), (0,)))
        grad_preact = (
            dot(grad_branch, weight_out[0], ((1,), (1,))) * slope0[cells, :].astype(F32)
        ).astype(BF16)
        bias_sum[...] += dot(owned(k, (8, chunk), 1).astype(BF16), grad_preact)
        in_sum[...] += dot(scaled, grad_preact, ((0,), (0,)))
        grad_scaled = dot(grad_preact, weight_in[0], ((1,), (1,)))
        rows_all[GAIN_ROW : GAIN_ROW + 1, :] += jnp.sum(
            grad_scaled * normed * mask, axis=0, keepdims=True
        )
        e = grad_scaled * gain_row
        grad = inv_std * (
            e
            - jnp.mean(e, axis=-1, keepdims=True)
            - normed * jnp.mean(e * normed, axis=-1, keepdims=True)
        )
        grad = grad.astype(BF16)
        grad0[cells, :] = grad
        g0_flat[cells, :] = grad.astype(F32)
        d1[cells, :] = upstream.astype(BF16)
        return carry

    lax.fori_loop(0, rim_rows // 2, block0, 0)

    join_rows(g_scratch, x_above, canon_x, x_below, WIDE * full, 0)
    tap_sums(
        g_scratch,
        full,
        RIM * full + RIM,
        g0_flat,
        slim,
        RIM * slim + RIM,
        height,
        width // 8,
        rows_all,
    )
    strips = big1.shape[1]
    pack_weights(in_sum, out_sum, weight_out[0], scale[0:1, :], packed, 0, rows_all)
    big_rows = big1.shape[2]
    packed[:, strips:, 0:big_rows, :] = big1[...]
    rows_all[half:, :] = rows1[...]
    rows_all[half : half + TAPS, :] = taps1[0:TAPS, :]
    small = rows_all[...].T
    members = packed.shape[0]
    part = channels // members
    zeros = jnp.zeros((8, channels), BF16)
    for d in range(members):
        for y in range(2 * strips):
            if y < part // 8:
                begin = d * part + 8 * y
                rows = small[begin : begin + 8, :].astype(BF16)
            elif y < part // 8 + 2:
                sums = bias_sum if y == part // 8 else bias1
                lane = (d // 2) * channels
                rows = sums[:, lane : lane + channels]
                if d % 2:
                    rows = pltpu.roll(rows, channels // 2, 1)
                rows = rows.astype(BF16)
            else:
                rows = zeros
            packed[d, y, big_rows : big_rows + 8, :] = rows


def spread_kernel(height, width, flip, tile, kernel, d1, grad0, grad_input, taps, g_flat, d_flat, out):
    slim = width + 8
    taps[0:TAPS, :] = kernel[0].astype(F32)
    g_flat[...] = grad0[...].astype(F32)
    d_flat[...] = d1[...].astype(F32)

    def emit(base, centers, sums):
        if sums is not None:
            for r in range(height):
                own = d_flat[pl.ds(base + ((r + RIM) * slim + RIM), 8), :]
                out[pl.ds(base + r * width, 8), :] = own + sums[r]

    convolve(g_flat, slim, taps, True, height, width // 8, emit)
    plain = turner(0, width).astype(F32)
    flipped = turner(1, width).astype(F32)
    for r in range(height):
        turn = jnp.where(row_flag(flip, tile, r, height, width) > 0, flipped, plain).astype(BF16)
        cells = slice(r * width, (r + 1) * width)
        grad_input[cells, :] = dot(turn, out[cells, :].astype(BF16)).astype(BF16)


def unpack_kernel(
    normalizer, full, tap_rows, gain_row, inward, bias, outward, scale_row
):
    layers, part, hidden = inward.shape
    channels = full.shape[2]
    strips = hidden // channels
    piece = outward.shape[1] // strips
    begin = part + piece
    for b in range(layers):
        for s in range(strips):
            block = full[b * strips + s, 0:begin, :].astype(F32) * normalizer
            inward[b, :, s * channels : (s + 1) * channels] = block[:part]
            outward[b, s * piece : (s + 1) * piece, :] = block[part:]
    chunks = part // 8
    small = jnp.concatenate([full[y, begin : begin + 8, :] for y in range(chunks)], axis=0)
    across = small.astype(F32) * normalizer
    small = across.T
    half = channels // layers
    for b in range(layers):
        tap_rows[b] = across[:, b * half : b * half + TAPS]
        gain_row[b : b + 1, :] = small[b * half + GAIN_ROW : b * half + GAIN_ROW + 1]
        scale_row[b : b + 1, :] = small[b * half + SCALE_ROW : b * half + SCALE_ROW + 1]
        rows = full[chunks + b, begin : begin + 8, :].astype(F32) * normalizer
        bias[b : b + 1, :] = rows[0:1, : bias.shape[1]]


def shape_of(*sizes, dtype=BF16):
    return jax.ShapeDtypeStruct(sizes, dtype)


def call(body, outs, flags=0, ins=0, scratch=(), cost=None):
    smem = pl.BlockSpec(memory_space=pltpu.SMEM)
    vmem = pl.BlockSpec(memory_space=pltpu.VMEM)
    return pl.pallas_call(
        body,
        out_shape=outs,
        in_specs=[smem] * flags + [vmem] * ins,
        out_specs=[vmem] * len(outs),
        scratch_shapes=[pltpu.VMEM(s, F32) for s in scratch],
        cost_estimate=cost,
        compiler_params=pltpu.CompilerParams(vmem_limit_bytes=LIMIT),
    )


def work(flops):
    return pl.CostEstimate(flops=flops, bytes_accessed=1 << 20, transcendentals=0)


def shifted(block, axis, distance):
    count = lax.axis_size(axis)
    return lax.ppermute(block, axis, [(i, (i + distance) % count) for i in range(count)])


def exchanged(blocks, axis):
    return lax.all_to_all(blocks, axis, 0, 0, tiled=True)


def summed_shares(packed, hidden):
    members, rows, _, channels = packed.shape
    part = channels // members
    layers = 2
    strips = rows // layers
    share = jnp.sum(exchanged(packed, DP).astype(F32), axis=0)
    piece = jnp.sum(exchanged(share.astype(BF16), "y").astype(F32), axis=0)
    others = lax.axis_size("zh") * lax.axis_size("c")
    copies = jnp.broadcast_to(piece.astype(BF16)[None], (others, *piece.shape))
    piece = jnp.sum(exchanged(copies, ("zh", "c")).astype(F32), axis=0)
    copies = jnp.broadcast_to(piece.astype(BF16)[None], (rows, *piece.shape))
    return exchanged(copies, "y")


def unpacked(full, normalizer, hidden, members):
    channels = full.shape[2]
    layers = 2
    part = channels // members
    row = shape_of(layers, part, dtype=F32)
    taps, *others = call(
        functools.partial(unpack_kernel, normalizer),
        [
            shape_of(layers, part, TAPS, dtype=F32),
            row,
            shape_of(layers, part, hidden, dtype=F32),
            shape_of(layers, hidden // members, dtype=F32),
            shape_of(layers, hidden // members, channels, dtype=F32),
            row,
        ],
        0,
        1,
    )(full)
    return (taps.transpose(0, 2, 1), *others)


def on_device(
    fields, cotangent, face_flip, kernel, ln_gain, weight_in, bias_in, weight_out, layer_scale
):
    height, width, channels = fields.shape[1:]
    hidden = weight_in.shape[2]
    members = lax.axis_size(DP)
    own, full, slim = height * width, width + 16, width + 8
    rim_rows = height + 2 * RIM
    rim = rim_rows * slim
    tall = (height + 2 * WIDE) * full
    sent = WIDE * full + RIM * slim
    strips = hidden // channels
    big_rows = channels // members + hidden // members // strips
    tile = lax.axis_index(TILE).astype(jnp.int32).reshape(1)

    cells = shape_of(own, channels)
    edges = shape_of(height * EDGE, channels)
    given = (face_flip, tile, fields.reshape(own, channels), cotangent.reshape(own, channels))
    east, west = call(functools.partial(edge_kernel, height, width), [edges, edges], 2, 2)(*given)
    canon, up = call(
        functools.partial(orient_kernel, height, width), [cells, cells], 2, 2, cost=work(own * 1024)
    )(*given)
    before = shifted(east, "zh", 1)
    after = shifted(west, "zh", -1)
    canon_x, up_x, to_next, to_prev = call(
        functools.partial(widen_kernel, height, width),
        [
            shape_of(height * full, channels),
            shape_of(height * slim, channels),
            shape_of(sent, channels),
            shape_of(sent, channels),
        ],
        0,
        4,
    )(before, after, canon, up)
    above = shifted(to_next, TILE, 1)
    below = shifted(to_prev, TILE, -1)
    sums = (channels, hidden)
    (
        result,
        conv0,
        slope0,
        hidden0,
        h1,
        grad_conv,
        east,
        west,
        scaled1,
        hidden1,
        grad_preact1,
        gain1,
    ) = call(
        functools.partial(forward_kernel, height, width),
        [
            cells,
            shape_of(rim, channels, dtype=F32),
            shape_of(rim, hidden),
            shape_of(rim, hidden),
            shape_of(rim, channels),
            cells,
            edges,
            edges,
            cells,
            shape_of(own, hidden),
            shape_of(own, hidden),
            shape_of(8, channels, dtype=F32),
        ],
        2,
        10,
        [
            (tall, channels),
            (56, channels),
            (rim, channels),
            (own, channels),
            (own, channels),
        ],
    )(
        face_flip,
        tile,
        above,
        canon_x,
        below,
        up,
        kernel,
        ln_gain,
        weight_in,
        bias_in,
        weight_out,
        layer_scale,
    )
    before = shifted(east, "zh", 1)
    after = shifted(west, "zh", -1)
    big1, bias1, rows1 = call(
        weights_kernel,
        [
            shape_of(members, strips, big_rows, channels),
            shape_of(8, hidden, dtype=F32),
            shape_of(64, channels, dtype=F32),
        ],
        0,
        7,
        [sums, sums],
        work(4 * own * hidden * channels),
    )(scaled1, hidden1, grad_preact1, up, gain1, weight_out, layer_scale)
    due, big1 = lax.optimization_barrier((grad_conv, big1))
    (taps1,) = call(
        functools.partial(taps_kernel, height, width),
        [shape_of(56, channels, dtype=F32)],
        0,
        2,
        [(rim, channels), (own, channels)],
        work(2 * TAPS * own * channels),
    )(h1, grad_conv)
    grad_x, to_next, to_prev = call(
        functools.partial(widen_grad_kernel, height, width),
        [
            shape_of(height * full, channels),
            shape_of(WIDE * full, channels),
            shape_of(WIDE * full, channels),
        ],
        0,
        3,
    )(before, after, due)
    grad_above = shifted(to_next, TILE, 1)
    grad_below = shifted(to_prev, TILE, -1)
    d1, grad0, packed = call(
        functools.partial(backward_kernel, height, width),
        [
            shape_of(rim, channels),
            shape_of(rim, channels),
            shape_of(members, 2 * strips, big_rows + 8, channels),
        ],
        0,
        19,
        [
            (tall, channels),
            (56, channels),
            (rim, channels),
            (rim, channels),
            (rim, channels),
            sums,
            sums,
            (8, hidden),
            (128, channels),
        ],
    )(
        grad_above,
        grad_x,
        grad_below,
        above,
        canon_x,
        below,
        up_x,
        kernel,
        ln_gain,
        weight_in,
        weight_out,
        layer_scale,
        conv0,
        slope0,
        hidden0,
        big1,
        bias1,
        rows1,
        taps1,
    )
    (grad_input,) = call(
        functools.partial(spread_kernel, height, width),
        [cells],
        2,
        3,
        [(56, channels), (rim, channels), (rim, channels), (own, channels)],
        work(2 * TAPS * own * channels),
    )(face_flip, tile, kernel, d1, grad0)
    normalizer = 1.0 / math.sqrt(members * 12 * width * width)
    shares = unpacked(summed_shares(packed, hidden), normalizer, hidden, members)
    return (result.reshape(fields.shape), grad_input.reshape(fields.shape), *shares)


def solution(mesh, sizes=(4, 8, 2, 2, 4)):
    mesh = jax.sharding.Mesh(mesh.devices.reshape(sizes), ("zh", "y", "c", "zl", "x"))
    return jax.shard_map(
        on_device,
        mesh=mesh,
        in_specs=(P(DP, TILE, None, None), P(DP, TILE, None, None)) + (P(),) * 7,
        out_specs=(
            P(DP, TILE, None, None),
            P(DP, TILE, None, None),
            P(None, None, DP),
            P(None, DP),
            P(None, DP, None),
            P(None, DP),
            P(None, DP, None),
            P(None, DP),
        ),
        check_vma=False,
    )
```

```python
import functools
import math

import jax
import jax.numpy as jnp
from jax import lax
from jax.experimental import pallas as pl
from jax.experimental.pallas import tpu as pltpu
from jax.sharding import PartitionSpec as P

KS = 7
TAPS = KS * KS
RIM = KS // 2
WIDE = 2 * RIM
TILE = ("zh", "y", "c")
DP = ("zl", "x")
FAR = 2 * WIDE
EDGE = 24
LIMIT = 24 << 20
LEAD_X, LEAD_1, LEAD_0 = FAR + 2, WIDE + 2, RIM
PAD_X, PAD_H, PAD_1, PAD_0 = 32, 24, 16, 8
EPSILON = 1e-06
SQRT_HALF = 0.7071067811865476
INV_ROOT_TWO_PI = 0.3989422804014327
F32 = jnp.float32
BF16 = jnp.bfloat16
GAIN_ROW = TAPS
SCALE_ROW = TAPS + 1


def dot(a, b, over=((1,), (0,))):
    return lax.dot_general(a, b, (over, ((), ())), preferred_element_type=F32)


def gelu_parts(preact):
    normal_cdf = 0.5 * (1.0 + lax.erf(preact * SQRT_HALF))
    return (
        preact * normal_cdf,
        normal_cdf + preact * jnp.exp(-0.5 * preact * preact) * INV_ROOT_TWO_PI,
    )


def picker(rows, columns, source_of):
    i = lax.broadcasted_iota(jnp.int32, (rows, columns), 0)
    j = lax.broadcasted_iota(jnp.int32, (rows, columns), 1)
    return jnp.where(j == source_of(i), 1.0, 0.0).astype(BF16)


def row_flag(flip_ref, tile_ref, row, height, width):
    place = tile_ref[0] * height + row
    column = lax.div(place, 3 * width)
    level = lax.div(lax.rem(place, 3 * width), width)
    return jnp.where(flip_ref[4 * level + column] > 0, 1, 0)


def turner(flag, width):
    return picker(width, width, lambda i: i + flag * (width - 1 - 2 * i))


def moments(convolved):
    average = jnp.mean(convolved, axis=-1, keepdims=True)
    centered = convolved - average
    inv_std = lax.rsqrt(jnp.mean(centered * centered, axis=-1, keepdims=True) + EPSILON)
    return centered * inv_std, inv_std


def tap_row(taps, t):
    return jnp.broadcast_to(taps[pl.ds(t, 1), :], (8, taps.shape[1]))


def convolve(source, width, taps, turned, rows, groups, emit, start=0):
    def group(q, carry):
        base = pl.multiple_of(q * 8, 8)
        sums = [None] * rows
        centers = [None] * rows
        for j in range(KS):
            weights = [
                tap_row(taps, TAPS - 1 - (KS * i + j) if turned else KS * i + j) for i in range(KS)
            ]
            for r in range(rows + KS - 1):
                cells = source[pl.ds(base + (r * width + j + start), 8), :]
                if j == RIM and 0 <= r - RIM < rows:
                    centers[r - RIM] = cells
                for i in range(KS):
                    out = r - i
                    if 0 <= out < rows:
                        term = cells * weights[i]
                        sums[out] = term if sums[out] is None else sums[out] + term
            if j == RIM:
                emit(base, centers, None)
        emit(base, None, sums)
        return carry

    lax.fori_loop(0, groups, group, 0)


def tap_sums(source, width, source_start, grad, grad_width, grad_start, rows, groups, out):
    for j in range(KS):

        def group(q, sums, j=j):
            base = pl.multiple_of(q * 8, 8)
            sums = list(sums)
            grads = [
                grad[pl.ds(base + (grad_start + r * grad_width), 8), :] for r in range(rows)
            ]
            for r in range(rows + KS - 1):
                cells = source[pl.ds(base + (source_start + r * width + j), 8), :]
                for i in range(KS):
                    if 0 <= r - i < rows:
                        sums[i] = sums[i] + cells * grads[r - i]
            return tuple(sums)

        zero = jnp.zeros((8, source.shape[1]), F32)
        sums = lax.fori_loop(0, groups, group, (zero,) * KS)
        for i in range(KS):
            out[pl.ds(KS * i + j, 1), :] = jnp.sum(sums[i], axis=0, keepdims=True)


def edge_kernel(height, width, flip, tile, fields, cotangent, east, west):
    far = 2 * width

    def turned(flag, i):
        return jnp.where(
            i >= width, width + i - width + flag * (3 * width - 1 - 2 * i), i + flag * (width - 1 - 2 * i)
        )

    def east_of(flag, i):
        place = jnp.where(i < FAR, width - FAR + i, far - WIDE + i - FAR)
        return jnp.where(i < FAR + WIDE, turned(flag, place), -1)

    def west_of(flag, i):
        place = jnp.where(i < FAR, i, width + i - FAR)
        return jnp.where(i < FAR + WIDE, turned(flag, place), -1)

    picks = []
    for flag in (0, 1):
        to_east = picker(EDGE, far, functools.partial(east_of, flag)).astype(F32)
        to_west = picker(EDGE, far, functools.partial(west_of, flag)).astype(F32)
        picks.append(jnp.concatenate([to_east, to_west], axis=0))
    for r in range(height):
        flag = row_flag(flip, tile, r, height, width)
        cells = slice(r * width, (r + 1) * width)
        both = jnp.concatenate([fields[cells, :], cotangent[cells, :]], axis=0)
        pick = jnp.where(flag > 0, picks[1], picks[0]).astype(BF16)
        edges = dot(pick, both).astype(BF16)
        edge = slice(r * EDGE, (r + 1) * EDGE)
        east[edge, :] = edges[:EDGE]
        west[edge, :] = edges[EDGE:]


def orient_kernel(height, width, flip, tile, fields, cotangent, canon, up):
    plain = turner(0, width).astype(F32)
    flipped = turner(1, width).astype(F32)
    for r in range(height):
        flag = row_flag(flip, tile, r, height, width)
        turn = jnp.where(flag > 0, flipped, plain).astype(BF16)
        cells = slice(r * width, (r + 1) * width)
        canon[cells, :] = dot(turn, fields[cells, :]).astype(BF16)
        up[cells, :] = dot(turn, cotangent[cells, :]).astype(BF16)


def widener(start, halo, lead, width, total):
    def source_of(i):
        c = i - lead
        inside = jnp.where(c < 0, start + halo + c, jnp.where(c < width, EDGE + c, EDGE + start + c))
        return jnp.where((c >= -halo) & (c < width + halo), inside, -1)

    return picker(total, width + 2 * EDGE, source_of)


def widen_kernel(
    height, width, before, after, canon, up, canon_x, up_1, up_0, to_next, to_prev
):
    pitch_x, pitch_1, pitch_0 = width + PAD_X, width + PAD_1, width + PAD_0
    pick_x = widener(0, FAR, LEAD_X, width, pitch_x)
    pick_1 = widener(FAR, WIDE, LEAD_1, width, pitch_1)
    pick_0 = widener(FAR, WIDE, LEAD_0, width, pitch_0)
    tail = WIDE * pitch_x
    for r in range(height):
        edge = slice(r * EDGE, (r + 1) * EDGE)
        cells = slice(r * width, (r + 1) * width)
        first, last = before[edge, :], after[edge, :]
        ups = jnp.concatenate([first, up[cells, :], last], axis=0)
        a = dot(pick_x, jnp.concatenate([first, canon[cells, :], last], axis=0)).astype(BF16)
        b = dot(pick_0, ups).astype(BF16)
        canon_x[r * pitch_x : (r + 1) * pitch_x, :] = a
        up_1[r * pitch_1 : (r + 1) * pitch_1, :] = dot(pick_1, ups).astype(BF16)
        up_0[r * pitch_0 : (r + 1) * pitch_0, :] = b
        if r < WIDE:
            to_prev[r * pitch_x : (r + 1) * pitch_x, :] = a
        if r < RIM:
            to_prev[tail + r * pitch_0 : tail + (r + 1) * pitch_0, :] = b
        if r >= height - WIDE:
            k = r - (height - WIDE)
            to_next[k * pitch_x : (k + 1) * pitch_x, :] = a
        if r >= height - RIM:
            k = r - (height - RIM)
            to_next[tail + k * pitch_0 : tail + (k + 1) * pitch_0, :] = b


def own_columns(shape, dim, rows, width):
    place = lax.broadcasted_iota(jnp.int32, shape, dim)
    pitch = width + PAD_1
    column = place
    for r in range(1, rows):
        column = column - jnp.where(place >= r * pitch, pitch, 0)
    return jnp.where((column >= LEAD_1) & (column < LEAD_1 + width), 1.0, 0.0)


def join_rows(target, above, middle, below, count, start):
    rows = middle.shape[0]
    target[0:count, :] = above[start : start + count, :].astype(F32)
    target[count : count + rows, :] = middle[...].astype(F32)
    target[count + rows : 2 * count + rows, :] = below[start : start + count, :].astype(F32)


def forward_kernel(
    height,
    width,
    flip,
    tile,
    above,
    canon_x,
    below,
    up,
    kernel,
    gain,
    weight_in,
    bias,
    weight_out,
    scale,
    result,
    conv0,
    slope0,
    hidden0,
    h1,
    grad_conv,
    to_next,
    to_prev,
    scaled1,
    hidden1,
    grad_preact1,
    gain_sum,
    x_scratch,
    taps,
    conv_flat,
    h1_flat,
    middle,
    conv1,
):
    pitch_x, pitch_h, pitch_1 = width + PAD_X, width + PAD_H, width + PAD_1
    pitch_0 = width + PAD_0
    rim_rows = height + 2 * RIM
    join_rows(x_scratch, above, canon_x, below, WIDE * pitch_x, 0)
    taps[0:TAPS, :] = kernel[0].astype(F32)

    def emit0(base, centers, sums):
        for r in range(rim_rows):
            if centers is not None:
                h1_flat[pl.ds(base + r * pitch_h, 8), :] = centers[r]
            else:
                conv_flat[pl.ds(base + r * pitch_h, 8), :] = sums[r]

    convolve(x_scratch, pitch_x, taps, False, rim_rows, pitch_h // 8, emit0)

    chunk0 = 2 * pitch_h
    skip = LEAD_X - RIM - LEAD_0

    def kept(array):
        rows = [array[r * pitch_h + skip : r * pitch_h + skip + pitch_0] for r in range(2)]
        return jnp.concatenate(rows, axis=0)

    def block0(k, carry):
        cells = pl.ds(pl.multiple_of(k * chunk0, 16), chunk0)
        saved = pl.ds(pl.multiple_of(k * 2 * pitch_0, 16), 2 * pitch_0)
        convolved = conv_flat[cells, :]
        conv0[saved, :] = kept(convolved)
        normed, _ = moments(convolved)
        scaled = (normed * gain[0:1, :]).astype(BF16)
        preact = dot(scaled, weight_in[0]) + bias[0:1, :]
        value, slope = gelu_parts(preact)
        slope0[saved, :] = kept(slope).astype(BF16)
        hidden0[saved, :] = kept(value).astype(BF16)
        branch = dot(value.astype(BF16), weight_out[0])
        state = (h1_flat[cells, :] + scale[0:1, :] * branch).astype(BF16)
        h1[cells, :] = state
        h1_flat[cells, :] = state.astype(F32)
        return carry

    lax.fori_loop(0, rim_rows // 2, block0, 0)

    taps[0:TAPS, :] = kernel[1].astype(F32)

    def emit1(base, centers, sums):
        for r in range(height):
            if centers is not None:
                middle[pl.ds(base + r * pitch_1, 8), :] = centers[r]
            else:
                conv1[pl.ds(base + r * pitch_1, 8), :] = sums[r]

    convolve(h1_flat, pitch_h, taps, False, height, pitch_1 // 8, emit1)

    gain_sum[...] = jnp.zeros_like(gain_sum)
    chunk_rows = 3
    chunk1 = chunk_rows * pitch_1
    plain = turner(0, width).astype(F32)
    flipped = turner(1, width).astype(F32)

    def block1(k, carry):
        cells = pl.ds(pl.multiple_of(k * chunk1, 8), chunk1)
        normed, inv_std = moments(conv1[cells, :])
        gain_row = gain[1:2, :]
        scaled = (normed * gain_row).astype(BF16)
        preact = dot(scaled, weight_in[1]) + bias[1:2, :]
        value, slope = gelu_parts(preact)
        hidden = value.astype(BF16)
        branch = dot(hidden, weight_out[1])
        scale_row = scale[1:2, :]
        state = middle[cells, :] + scale_row * branch
        upstream = up[cells, :]
        grad_branch = (upstream.astype(F32) * scale_row).astype(BF16)
        grad_preact = (dot(grad_branch, weight_out[1], ((1,), (1,))) * slope).astype(BF16)
        scaled1[cells, :] = scaled
        hidden1[cells, :] = hidden
        grad_preact1[cells, :] = grad_preact
        grad_scaled = dot(grad_preact, weight_in[1], ((1,), (1,)))
        gain_sum[0:1, :] += jnp.sum(
            grad_scaled * normed * own_columns(normed.shape, 0, chunk_rows, width),
            axis=0,
            keepdims=True,
        )
        e = grad_scaled * gain_row
        grad = inv_std * (
            e
            - jnp.mean(e, axis=-1, keepdims=True)
            - normed * jnp.mean(e * normed, axis=-1, keepdims=True)
        )
        grad_conv[cells, :] = grad.astype(BF16)
        for r in range(chunk_rows):
            row = k * chunk_rows + r
            flag = row_flag(flip, tile, row, height, width)
            turn = jnp.where(flag > 0, flipped, plain).astype(BF16)
            own = state[r * pitch_1 + LEAD_1 : r * pitch_1 + LEAD_1 + width].astype(BF16)
            result[pl.ds(pl.multiple_of(row * width, 8), width), :] = dot(turn, own).astype(BF16)
        return carry

    lax.fori_loop(0, height // chunk_rows, block1, 0)
    rows = to_prev.shape[0]
    to_prev[...] = grad_conv[0:rows, :]
    to_next[...] = grad_conv[height * pitch_1 - rows : height * pitch_1, :]


def weights_kernel(
    height, width, scaled, hidden, grad_preact, up, gain_sum, weight_out, scale, big, bias_sum, rows_out, in_sum, out_sum
):
    in_sum[...] = jnp.zeros_like(in_sum)
    out_sum[...] = jnp.zeros_like(out_sum)
    bias_sum[...] = jnp.zeros_like(bias_sum)
    rows_out[...] = jnp.zeros_like(rows_out)
    steps = 3
    chunk = scaled.shape[0] // steps
    rows = height // steps
    ones = own_columns((8, chunk), 1, rows, width).astype(BF16)
    mask = own_columns((chunk, scaled.shape[1]), 0, rows, width)

    def owned(array):
        return (array.astype(F32) * mask).astype(BF16)

    def step(k, carry):
        cells = pl.ds(pl.multiple_of(k * chunk, 8), chunk)
        out_sum[...] += dot(owned(up[cells, :]), hidden[cells, :], ((0,), (0,)))
        bias_sum[...] += dot(ones, grad_preact[cells, :])
        in_sum[...] += dot(owned(scaled[cells, :]), grad_preact[cells, :], ((0,), (0,)))
        return carry

    lax.fori_loop(0, steps, step, 0)
    rows_out[GAIN_ROW : GAIN_ROW + 1, :] = gain_sum[0:1, :]
    pack_weights(in_sum, out_sum, weight_out[1], scale[1:2, :], big, 0, rows_out)


def pack_weights(in_sum, out_sum, weight_out, scale_row, big, first, rows_out):
    channels = in_sum.shape[0]
    members = big.shape[0]
    part = channels // members
    products = out_sum[...].T
    rows_out[SCALE_ROW : SCALE_ROW + 1, :] = jnp.sum(
        products * weight_out.astype(F32), axis=0, keepdims=True
    )
    outward = products * scale_row
    strips = in_sum.shape[1] // channels
    share = outward.shape[0] // members
    piece = share // strips
    for d in range(members):
        for s in range(strips):
            big[d, first + s, 0:part, :] = in_sum[
                d * part : (d + 1) * part, s * channels : (s + 1) * channels
            ].astype(BF16)
            begin = d * share + s * piece
            big[d, first + s, part : part + piece, :] = outward[begin : begin + piece, :].astype(
                BF16
            )


def taps_kernel(height, width, h1, grad_conv, out, source, grad):
    source[...] = h1[...].astype(F32)
    grad[...] = grad_conv[...].astype(F32)
    tap_sums(
        source, width + PAD_H, LEAD_1, grad, width + PAD_1, LEAD_1, height, width // 8, out
    )


def backward_kernel(
    height,
    width,
    above,
    grad_x,
    below,
    x_above,
    canon_x,
    x_below,
    up_x,
    kernel,
    gain,
    weight_in,
    weight_out,
    scale,
    conv0,
    slope0,
    hidden0,
    big1,
    bias1,
    rows1,
    taps1,
    d1,
    grad0,
    packed,
    g_scratch,
    taps,
    up_flat,
    d_flat,
    g0_flat,
    in_sum,
    out_sum,
    bias_sum,
    rows_all,
):
    full, slim, pitch_1 = width + PAD_X, width + PAD_0, width + PAD_1
    rim_rows = height + 2 * RIM
    channels = gain.shape[1]
    join_rows(g_scratch, above, grad_x, below, WIDE * pitch_1, 0)
    join_rows(up_flat, x_above, up_x, x_below, RIM * slim, WIDE * full)
    taps[0:TAPS, :] = kernel[1].astype(F32)

    def emit1(base, centers, sums):
        if sums is not None:
            for r in range(rim_rows):
                cells = pl.ds(base + r * slim, 8)
                d_flat[cells, :] = (up_flat[cells, :] + sums[r]).astype(BF16).astype(F32)

    convolve(
        g_scratch, pitch_1, taps, True, rim_rows, slim // 8, emit1, LEAD_1 - LEAD_0 - RIM
    )

    in_sum[...] = jnp.zeros_like(in_sum)
    out_sum[...] = jnp.zeros_like(out_sum)
    bias_sum[...] = jnp.zeros_like(bias_sum)
    rows_all[...] = jnp.zeros_like(rows_all)
    half = rows1.shape[0]
    chunk = 2 * slim

    def owned(k, shape, dim):
        place = lax.broadcasted_iota(jnp.int32, shape, dim)
        second = jnp.where(place >= slim, 1, 0)
        row = 2 * k + second
        column = place - slim * second
        inside = (
            (row >= RIM) & (row < RIM + height) & (column >= RIM) & (column < RIM + width)
        )
        return jnp.where(inside, 1.0, 0.0)

    def block0(k, carry):
        cells = pl.ds(pl.multiple_of(k * chunk, 16), chunk)
        mask = owned(k, (chunk, channels), 0)
        normed, inv_std = moments(conv0[cells, :])
        gain_row = gain[0:1, :]
        scaled = (normed * gain_row * mask).astype(BF16)
        upstream = d_flat[cells, :]
        grad_branch = (upstream * scale[0:1, :]).astype(BF16)
        out_sum[...] += dot((upstream * mask).astype(BF16), hidden0[cells, :], ((0,), (0,)))
        grad_preact = (
            dot(grad_branch, weight_out[0], ((1,), (1,))) * slope0[cells, :].astype(F32)
        ).astype(BF16)
        bias_sum[...] += dot(owned(k, (8, chunk), 1).astype(BF16), grad_preact)
        in_sum[...] += dot(scaled, grad_preact, ((0,), (0,)))
        grad_scaled = dot(grad_preact, weight_in[0], ((1,), (1,)))
        rows_all[GAIN_ROW : GAIN_ROW + 1, :] += jnp.sum(
            grad_scaled * normed * mask, axis=0, keepdims=True
        )
        e = grad_scaled * gain_row
        grad = inv_std * (
            e
            - jnp.mean(e, axis=-1, keepdims=True)
            - normed * jnp.mean(e * normed, axis=-1, keepdims=True)
        )
        grad = grad.astype(BF16)
        grad0[cells, :] = grad
        g0_flat[cells, :] = grad.astype(F32)
        d1[cells, :] = upstream.astype(BF16)
        return carry

    lax.fori_loop(0, rim_rows // 2, block0, 0)

    join_rows(g_scratch, x_above, canon_x, x_below, WIDE * full, 0)
    tap_sums(
        g_scratch,
        full,
        RIM * full + LEAD_X - RIM,
        g0_flat,
        slim,
        RIM * slim + RIM,
        height,
        width // 8,
        rows_all,
    )
    strips = big1.shape[1]
    pack_weights(in_sum, out_sum, weight_out[0], scale[0:1, :], packed, 0, rows_all)
    big_rows = big1.shape[2]
    packed[:, strips:, 0:big_rows, :] = big1[...]
    rows_all[half:, :] = rows1[...]
    rows_all[half : half + TAPS, :] = taps1[0:TAPS, :]
    small = rows_all[...].T
    members = packed.shape[0]
    part = channels // members
    zeros = jnp.zeros((8, channels), BF16)
    for d in range(members):
        for y in range(2 * strips):
            if y < part // 8:
                begin = d * part + 8 * y
                rows = small[begin : begin + 8, :].astype(BF16)
            elif y < part // 8 + 2:
                sums = bias_sum if y == part // 8 else bias1
                lane = (d // 2) * channels
                rows = sums[:, lane : lane + channels]
                if d % 2:
                    rows = pltpu.roll(rows, channels // 2, 1)
                rows = rows.astype(BF16)
            else:
                rows = zeros
            packed[d, y, big_rows : big_rows + 8, :] = rows


def spread_kernel(height, width, flip, tile, kernel, d1, grad0, grad_input, taps, g_flat, d_flat, out):
    slim = width + 8
    taps[0:TAPS, :] = kernel[0].astype(F32)
    g_flat[...] = grad0[...].astype(F32)
    d_flat[...] = d1[...].astype(F32)

    def emit(base, centers, sums):
        if sums is not None:
            for r in range(height):
                own = d_flat[pl.ds(base + ((r + RIM) * slim + RIM), 8), :]
                out[pl.ds(base + r * width, 8), :] = own + sums[r]

    convolve(g_flat, slim, taps, True, height, width // 8, emit)
    plain = turner(0, width).astype(F32)
    flipped = turner(1, width).astype(F32)
    for r in range(height):
        turn = jnp.where(row_flag(flip, tile, r, height, width) > 0, flipped, plain).astype(BF16)
        cells = slice(r * width, (r + 1) * width)
        grad_input[cells, :] = dot(turn, out[cells, :].astype(BF16)).astype(BF16)


def unpack_kernel(
    normalizer, full, tap_rows, gain_row, inward, bias, outward, scale_row
):
    layers, part, hidden = inward.shape
    channels = full.shape[2]
    strips = hidden // channels
    piece = outward.shape[1] // strips
    begin = part + piece
    for b in range(layers):
        for s in range(strips):
            block = full[b * strips + s, 0:begin, :].astype(F32) * normalizer
            inward[b, :, s * channels : (s + 1) * channels] = block[:part]
            outward[b, s * piece : (s + 1) * piece, :] = block[part:]
    chunks = part // 8
    small = jnp.concatenate([full[y, begin : begin + 8, :] for y in range(chunks)], axis=0)
    across = small.astype(F32) * normalizer
    small = across.T
    half = channels // layers
    for b in range(layers):
        tap_rows[b] = across[:, b * half : b * half + TAPS]
        gain_row[b : b + 1, :] = small[b * half + GAIN_ROW : b * half + GAIN_ROW + 1]
        scale_row[b : b + 1, :] = small[b * half + SCALE_ROW : b * half + SCALE_ROW + 1]
        rows = full[chunks + b, begin : begin + 8, :].astype(F32) * normalizer
        bias[b : b + 1, :] = rows[0:1, : bias.shape[1]]


def shape_of(*sizes, dtype=BF16):
    return jax.ShapeDtypeStruct(sizes, dtype)


def call(body, outs, flags=0, ins=0, scratch=(), cost=None):
    smem = pl.BlockSpec(memory_space=pltpu.SMEM)
    vmem = pl.BlockSpec(memory_space=pltpu.VMEM)
    return pl.pallas_call(
        body,
        out_shape=outs,
        in_specs=[smem] * flags + [vmem] * ins,
        out_specs=[vmem] * len(outs),
        scratch_shapes=[pltpu.VMEM(s, F32) for s in scratch],
        cost_estimate=cost,
        compiler_params=pltpu.CompilerParams(vmem_limit_bytes=LIMIT),
    )


def work(flops):
    return pl.CostEstimate(flops=flops, bytes_accessed=1 << 20, transcendentals=0)


def shifted(block, axis, distance):
    count = lax.axis_size(axis)
    return lax.ppermute(block, axis, [(i, (i + distance) % count) for i in range(count)])


def exchanged(blocks, axis):
    return lax.all_to_all(blocks, axis, 0, 0, tiled=True)


def summed_shares(packed, hidden):
    members, rows, _, channels = packed.shape
    part = channels // members
    layers = 2
    strips = rows // layers
    share = jnp.sum(exchanged(packed, DP).astype(F32), axis=0)
    piece = jnp.sum(exchanged(share.astype(BF16), "y").astype(F32), axis=0)
    others = lax.axis_size("zh") * lax.axis_size("c")
    copies = jnp.broadcast_to(piece.astype(BF16)[None], (others, *piece.shape))
    piece = jnp.sum(exchanged(copies, ("zh", "c")).astype(F32), axis=0)
    copies = jnp.broadcast_to(piece.astype(BF16)[None], (rows, *piece.shape))
    return exchanged(copies, "y")


def unpacked(full, normalizer, hidden, members):
    channels = full.shape[2]
    layers = 2
    part = channels // members
    row = shape_of(layers, part, dtype=F32)
    taps, *others = call(
        functools.partial(unpack_kernel, normalizer),
        [
            shape_of(layers, part, TAPS, dtype=F32),
            row,
            shape_of(layers, part, hidden, dtype=F32),
            shape_of(layers, hidden // members, dtype=F32),
            shape_of(layers, hidden // members, channels, dtype=F32),
            row,
        ],
        0,
        1,
    )(full)
    return (taps.transpose(0, 2, 1), *others)


def on_device(
    fields, cotangent, face_flip, kernel, ln_gain, weight_in, bias_in, weight_out, layer_scale
):
    height, width, channels = fields.shape[1:]
    hidden = weight_in.shape[2]
    members = lax.axis_size(DP)
    own, full, slim = height * width, width + PAD_X, width + PAD_0
    pitch_h, pitch_1 = width + PAD_H, width + PAD_1
    rim_rows = height + 2 * RIM
    rim = rim_rows * slim
    tall = (height + 2 * WIDE) * full
    sent = WIDE * full + RIM * slim
    strips = hidden // channels
    big_rows = channels // members + hidden // members // strips
    tile = lax.axis_index(TILE).astype(jnp.int32).reshape(1)

    cells = shape_of(own, channels)
    cells_1 = shape_of(height * pitch_1, channels)
    edges = shape_of(height * EDGE, channels)
    given = (face_flip, tile, fields.reshape(own, channels), cotangent.reshape(own, channels))
    east, west = call(functools.partial(edge_kernel, height, width), [edges, edges], 2, 2)(*given)
    canon, up = call(
        functools.partial(orient_kernel, height, width), [cells, cells], 2, 2, cost=work(own * 1024)
    )(*given)
    before = shifted(east, "zh", 1)
    after = shifted(west, "zh", -1)
    canon_x, up_1, up_0, to_next, to_prev = call(
        functools.partial(widen_kernel, height, width),
        [
            shape_of(height * full, channels),
            shape_of(height * pitch_1, channels),
            shape_of(height * slim, channels),
            shape_of(sent, channels),
            shape_of(sent, channels),
        ],
        0,
        4,
    )(before, after, canon, up)
    above = shifted(to_next, TILE, 1)
    below = shifted(to_prev, TILE, -1)
    sums = (channels, hidden)
    (
        result,
        conv0,
        slope0,
        hidden0,
        h1,
        grad_conv,
        to_next,
        to_prev,
        scaled1,
        hidden1,
        grad_preact1,
        gain1,
    ) = call(
        functools.partial(forward_kernel, height, width),
        [
            cells,
            shape_of(rim, channels, dtype=F32),
            shape_of(rim, hidden),
            shape_of(rim, hidden),
            shape_of(rim_rows * pitch_h, channels),
            cells_1,
            shape_of(WIDE * pitch_1, channels),
            shape_of(WIDE * pitch_1, channels),
            cells_1,
            shape_of(height * pitch_1, hidden),
            shape_of(height * pitch_1, hidden),
            shape_of(8, channels, dtype=F32),
        ],
        2,
        10,
        [
            (tall, channels),
            (56, channels),
            (rim_rows * pitch_h, channels),
            (rim_rows * pitch_h, channels),
            (height * pitch_1, channels),
            (height * pitch_1, channels),
        ],
    )(
        face_flip,
        tile,
        above,
        canon_x,
        below,
        up_1,
        kernel,
        ln_gain,
        weight_in,
        bias_in,
        weight_out,
        layer_scale,
    )
    big1, bias1, rows1 = call(
        functools.partial(weights_kernel, height, width),
        [
            shape_of(members, strips, big_rows, channels),
            shape_of(8, hidden, dtype=F32),
            shape_of(64, channels, dtype=F32),
        ],
        0,
        7,
        [sums, sums],
        work(4 * own * hidden * channels),
    )(scaled1, hidden1, grad_preact1, up_1, gain1, weight_out, layer_scale)
    (taps1,) = call(
        functools.partial(taps_kernel, height, width),
        [shape_of(56, channels, dtype=F32)],
        0,
        2,
        [(rim_rows * pitch_h, channels), (height * pitch_1, channels)],
        work(2 * TAPS * own * channels),
    )(h1, grad_conv)
    grad_above = shifted(to_next, TILE, 1)
    grad_below = shifted(to_prev, TILE, -1)
    d1, grad0, packed = call(
        functools.partial(backward_kernel, height, width),
        [
            shape_of(rim, channels),
            shape_of(rim, channels),
            shape_of(members, 2 * strips, big_rows + 8, channels),
        ],
        0,
        19,
        [
            (tall, channels),
            (56, channels),
            (rim, channels),
            (rim, channels),
            (rim, channels),
            sums,
            sums,
            (8, hidden),
            (128, channels),
        ],
    )(
        grad_above,
        grad_conv,
        grad_below,
        above,
        canon_x,
        below,
        up_0,
        kernel,
        ln_gain,
        weight_in,
        weight_out,
        layer_scale,
        conv0,
        slope0,
        hidden0,
        big1,
        bias1,
        rows1,
        taps1,
    )
    (grad_input,) = call(
        functools.partial(spread_kernel, height, width),
        [cells],
        2,
        3,
        [(56, channels), (rim, channels), (rim, channels), (own, channels)],
        work(2 * TAPS * own * channels),
    )(face_flip, tile, kernel, d1, grad0)
    normalizer = 1.0 / math.sqrt(members * 12 * width * width)
    shares = unpacked(summed_shares(packed, hidden), normalizer, hidden, members)
    return (result.reshape(fields.shape), grad_input.reshape(fields.shape), *shares)


def solution(mesh, sizes=(4, 8, 2, 2, 4)):
    mesh = jax.sharding.Mesh(mesh.devices.reshape(sizes), ("zh", "y", "c", "zl", "x"))
    return jax.shard_map(
        on_device,
        mesh=mesh,
        in_specs=(P(DP, TILE, None, None), P(DP, TILE, None, None)) + (P(),) * 7,
        out_specs=(
            P(DP, TILE, None, None),
            P(DP, TILE, None, None),
            P(None, None, DP),
            P(None, DP),
            P(None, DP, None),
            P(None, DP),
            P(None, DP, None),
            P(None, DP),
        ),
        check_vma=False,
    )
```
